32 devices in a mesh: group: 4 (over y, x), tensor: 8 (over z, core).
Axes of the slice: x: 2, y: 2, z: 4, core: 2. Of those that a mesh axis runs over, the one named last changes fastest.
Arguments:
- prefill_states: bfloat16 [16384, 8192], P('group', 'tensor'), may hold values from -6 to 6
- key_weight: bfloat16 [8192, 1024], P('tensor'), may hold values from -0.0625 to 0.0625
- value_weight: bfloat16 [8192, 1024], P('tensor'), may hold values from -0.0625 to 0.0625
- page_slot: int32 [4, 8, 64], P('group', 'tensor'), may hold values from 0 to 63, each once within a row
- decode_states: bfloat16 [16, 8192], P('group'), may hold values from -6 to 6
- query_weight: bfloat16 [8192, 8192], P(None, 'tensor'), may hold values from -0.0625 to 0.0625
- cache_keys: bfloat16 [16, 4096, 1024], P('group', 'tensor'), may hold values from -606 to 606
- cache_values: bfloat16 [16, 4096, 1024], P('group', 'tensor'), may hold values from -6 to 6
- cached_length: int32 [16], P('group'), may hold values from 1 to 4096
Outputs:
- attention_out: bfloat16 [16, 8192], P('group', 'tensor')
The draws below stay inside these ranges and needn't reach their ends.
Inputs may be any that keep to these rules, and one draw needn't show every extreme that they name: For every group g and block t, page_slot[g, t, :] is a permutation of 0 to 63.
All inputs are finite; a program needn't handle non-finite values.
Results may differ from the reference program's by a relative error of at most 0.017.
Values may be sent and summed in bfloat16 or wider, within the bound.
A program may use at most 192 MiB of HBM per device.

```python
import jax
import jax.numpy as jnp
from jax import lax

D = 8192
QUERY_HEAD_COUNT = 64
KEY_VALUE_HEADS = 8
HEAD_WIDTH = 128
PAGE = 8
PRE_TOK = 4096
B_DEV = 4
KVW = 1024
QW = 8192
GROUPS = 4
RANKS = 8
PRE_ALL = 16384
DECODE_BATCH = 16
CONTEXT = 4096
PAGES_DEV = 64
PER_OWNER = 16
FRESH_ROW = 128
N_GROUP = 4
N_TENSOR = 8


def draw_cache_keys(key, part):
    normal_key = jax.random.fold_in(key, 0)
    base_draw = jnp.clip(jax.random.normal(normal_key, (DECODE_BATCH, CONTEXT, KVW), jnp.float32), -6.0, 6.0)
    return base_draw.astype(jnp.bfloat16)


def set_ends(values, key, low, top_value):
    shape = values.shape
    spot = [jax.random.randint(jax.random.fold_in(key, axis), (), 0, shape[axis]) for axis in range(len(shape))]
    values = values.at[tuple(spot)].set(low)
    longest = shape.index(max(shape))
    spot[longest] = (spot[longest] + 1) % shape[longest]
    return values.at[tuple(spot)].set(top_value)


def block_scale(rng, shape, pieces, smallest, high):
    factor_of, own = 1.0, jax.random.fold_in(rng, 6)
    for position, parts in pieces:
        heights = jnp.exp(jax.random.uniform(jax.random.fold_in(own, position), (parts,), jnp.float32, smallest / len(pieces), high / len(pieces)))
        factor_of = factor_of * jnp.repeat(heights, shape[position] // parts).reshape([-1 if axis == position else 1 for axis in range(len(shape))])
    return factor_of


def bell_draw(key, extent, width, reach, pieces=(), kind=jnp.bfloat16):
    result = jax.random.normal(key, extent, jnp.float32) * width
    if len(pieces) > 0:
        result = block_scale(key, extent, pieces, -0.22, 0.18) * result
    return jnp.clip(result, min=-reach, max=reach).astype(kind)


def setup_inputs(seed: int = 0) -> dict:
    arg_keys = jax.random.split(jax.random.key(seed), 10)
    return {
        "prefill_states": bell_draw(arg_keys[0], (PRE_ALL, D), 1.0, 6.0, ((0, 4), (1, 8))),
        "key_weight": bell_draw(arg_keys[1], (D, KVW), D ** -0.5, 0.0625, ((0, 8),)),
        "value_weight": bell_draw(arg_keys[2], (D, KVW), D ** -0.5, 0.0625, ((0, 8),)),
        "page_slot": jax.vmap(lambda own: jax.random.permutation(own, PAGES_DEV))(jax.random.split(arg_keys[3], GROUPS * RANKS)).reshape((GROUPS, RANKS, PAGES_DEV)).astype(jnp.int32),
        "decode_states": bell_draw(arg_keys[4], (DECODE_BATCH, D), 1.0, 6.0, ((0, 4),)),
        "query_weight": bell_draw(arg_keys[5], (D, QW), D ** -0.5, 0.0625, ((1, 8),)),
        "cache_keys": draw_cache_keys(jax.random.fold_in(arg_keys[9], 71), 0),
        "cache_values": bell_draw(arg_keys[7], (DECODE_BATCH, CONTEXT, KVW), 1.0, 6.0, ((0, 4), (1, 8))),
        "cached_length": set_ends(jax.random.randint(arg_keys[8], (DECODE_BATCH,), 1, CONTEXT + 1), jax.random.fold_in(arg_keys[8], 1), 1, CONTEXT).astype(jnp.int32),
    }


rope_theta = 500000.0
masked_score = -1e30


def apply_rotary(vectors, positions):
    half_width = vectors.shape[-1] // 2
    index_float = jnp.arange(half_width, dtype=jnp.float32)
    frequency = rope_theta ** (-2.0 * index_float / vectors.shape[-1])
    angles = positions[..., None].astype(jnp.float32) * frequency
    cosine_part = jnp.cos(angles)
    sine_part = jnp.sin(angles)
    first_half = vectors[..., :half_width]
    second_half = vectors[..., half_width:]
    return jnp.concatenate([first_half * cosine_part - second_half * sine_part, second_half * cosine_part + first_half * sine_part], axis=-1)


def reference(prefill_states, key_weight, value_weight, page_slot, decode_states, query_weight, cache_keys, cache_values, cached_length):
    def project(states):
        key_proj = jnp.dot(states, key_weight, preferred_element_type=jnp.float32)
        value_proj = jnp.dot(states, value_weight, preferred_element_type=jnp.float32)
        return key_proj.astype(jnp.bfloat16), value_proj.astype(jnp.bfloat16)

    fresh_keys, fresh_values = lax.map(project, prefill_states.reshape(N_GROUP, PRE_TOK, D))
    inverse = jnp.argsort(page_slot, axis=-1).astype(jnp.int32)

    def to_owners(fresh_rows):
        page_blocks = fresh_rows.reshape(N_GROUP, N_TENSOR, PAGES_DEV, PAGE * KVW)
        ordered = jnp.take_along_axis(page_blocks, inverse[..., None], axis=2)
        ordered = ordered.reshape(N_GROUP, N_TENSOR, N_GROUP, PER_OWNER * PAGE * KVW).transpose(2, 1, 0, 3)
        ordered = ordered.reshape(N_GROUP, N_TENSOR, B_DEV, FRESH_ROW, KVW).transpose(0, 2, 1, 3, 4)
        return ordered.reshape(DECODE_BATCH, N_TENSOR * FRESH_ROW, KVW)

    keys_in_place = to_owners(fresh_keys)
    owner_values = to_owners(fresh_values)
    fresh_length = N_TENSOR * FRESH_ROW
    fresh_position_index = cached_length[:, None] + jnp.arange(fresh_length, dtype=jnp.int32)[None, :]
    keys_by_owner = apply_rotary(keys_in_place.astype(jnp.float32).reshape(DECODE_BATCH, fresh_length, KEY_VALUE_HEADS, HEAD_WIDTH), fresh_position_index[:, :, None])
    keys_by_owner = keys_by_owner.reshape(DECODE_BATCH, fresh_length, KVW).astype(jnp.bfloat16)
    query_vectors = jnp.dot(decode_states, query_weight, preferred_element_type=jnp.float32).reshape(DECODE_BATCH, QUERY_HEAD_COUNT, HEAD_WIDTH)
    query_vectors = apply_rotary(query_vectors, (cached_length + fresh_length)[:, None]).astype(jnp.bfloat16).reshape(DECODE_BATCH, KEY_VALUE_HEADS, QUERY_HEAD_COUNT // KEY_VALUE_HEADS, HEAD_WIDTH)

    def attend(inputs):
        query_row, prior_keys, prior_values, incoming_keys, incoming_values, length = inputs
        key_row_block = jnp.concatenate([prior_keys, incoming_keys], axis=0).reshape(-1, KEY_VALUE_HEADS, HEAD_WIDTH).astype(jnp.float32)
        value_row_block = jnp.concatenate([prior_values, incoming_values], axis=0).reshape(-1, KEY_VALUE_HEADS, HEAD_WIDTH).astype(jnp.float32)
        scores = jnp.einsum("hgd,lhd->hgl", query_row.astype(jnp.float32), key_row_block) / (HEAD_WIDTH ** 0.5)
        usable = jnp.concatenate([jnp.arange(CONTEXT, dtype=jnp.int32) < length, jnp.ones((fresh_length,), dtype=bool)])
        scores = jnp.where(usable, scores, masked_score)
        row_peak = jnp.max(scores, axis=-1, keepdims=True)
        weights = jnp.exp(scores - row_peak)
        row_total = jnp.sum(weights, axis=-1)
        rounded = lax.optimization_barrier(weights.astype(jnp.bfloat16)).astype(jnp.float32)
        blended = jnp.einsum("hgl,lhd->hgd", rounded, value_row_block) / row_total[..., None]
        return blended.reshape(QW).astype(jnp.bfloat16)

    return lax.map(attend, (query_vectors, cache_keys, cache_values, keys_by_owner, owner_values, cached_length))
```

```python
import functools
import math

import jax
import jax.numpy as jnp
from jax import lax
from jax.experimental import pallas as pl
from jax.experimental.pallas import tpu as pltpu
from jax.sharding import PartitionSpec as P

HEAD_WIDTH = 128
PAGE = 8
FOLD = 16
CHUNKS = 4
PARTS = 2

rope_theta = 500000.0
masked_score = -1e30
F32, BF16 = jnp.float32, jnp.bfloat16


def log2_of(number):
    power = number.bit_length() - 1
    assert 1 << power == number
    return power


def remote(src, dst, send_sem, recv_sem, group, rank):
    return pltpu.make_async_remote_copy(
        src_ref=src,
        dst_ref=dst,
        send_sem=send_sem,
        recv_sem=recv_sem,
        device_id={"group": group, "tensor": rank},
        device_id_type=pl.DeviceIdType.MESH,
    )


def stack(pieces):
    return pieces[0] if len(pieces) == 1 else jnp.concatenate(pieces, axis=0)


def beside(pieces):
    return pieces[0] if len(pieces) == 1 else jnp.concatenate(pieces, axis=1)


def fold(values):
    count = FOLD // values.shape[0]
    width = values.shape[1] // count
    return stack([values[:, q * width : (q + 1) * width] for q in range(count)])


def unfold(values, height):
    return beside([values[q : q + height] for q in range(0, FOLD, height)])


def iota(shape, axis):
    return lax.broadcasted_iota(jnp.int32, shape, axis)


def body(
    groups, ranks,
    states, key_weight, value_weight, page_slot, decode, query_weight, cache_keys, cache_values,
    cached_length,
    out,
    x, wk, wv, wq, old_keys, old_values, slot_in, decode_in, lengths,
    fold_wide, decode_out, decode_all, slots, page_cos, page_sin, slot_of,
    query_part, query_in, query_all, spread, keys,
    partial, paired, chip_sums, incoming, own_sums,
    weights, peaks, totals, masked, mixed, fresh_out, fresh_in,
    old_wide, old_out, old_in, old_stat_out, old_stat_in, cross_out, cross_in,
    x_sems, load_sems,
    send_slot, got_slot, send_decode, got_decode, send_part, got_part, send_query, got_query,
    send_pair, got_pair, send_sum, got_sum, send_weight, send_on, got_weight,
    send_fresh, got_fresh, send_old, got_old, send_stat, got_stat, send_cross, got_cross,
):
    group, rank = lax.axis_index("group"), lax.axis_index("tensor")
    chips = ranks // 2
    core, chip = lax.rem(rank, 2), rank // 2
    partner = chip * 2 + 1 - core
    tokens, features = x.shape
    block = tokens // ranks
    pages = block // PAGE
    per_owner = pages // groups
    rows, context_dev, kv_width = old_keys.shape
    kv_heads = kv_width // HEAD_WIDTH
    local_heads = out.shape[1]
    heads = local_heads * ranks
    per_kv = heads // kv_heads
    share, span = block // groups, block // rows
    senders = span // share
    offset = lax.rem(group, senders) * share
    query_rows = query_part.shape[1]
    depth = wq.shape[0]
    pieces = FOLD // rows
    piece = depth // pieces
    chunk = tokens // CHUNKS
    per_chunk = chunk // block
    part = tokens // PARTS
    per_part = CHUNKS // PARTS
    log_scale = math.log2(math.e) / HEAD_WIDTH**0.5
    half = HEAD_WIDTH // 2

    def rank_at(step):
        return lax.rem(rank + step, ranks)

    def group_at(step):
        return lax.rem(group + step, groups)

    def chip_at(step):
        other = lax.rem(chip + step, chips)
        return other, other * 2 + core

    def x_copy(step):
        start = pl.ds(pl.multiple_of(step * block, block), block)
        return pltpu.make_async_copy(states.at[start, :], x.at[start, :], x_sems.at[step])

    def load(source, target, index):
        return pltpu.make_async_copy(source, target, load_sems.at[index])

    key_load = load(key_weight, wk, 0)
    slot_load = load(page_slot, slot_in, 1)
    decode_load = load(decode, decode_in, 2)
    length_load = load(cached_length, lengths, 3)
    query_load = load(
        query_weight.at[pl.ds(pl.multiple_of(group * depth, depth), depth), :], wq, 4
    )
    value_load = load(value_weight, wv, 5)
    old_key_load = load(cache_keys, old_keys, 6)
    old_value_load = load(cache_values, old_values, 7)

    slot_load.start()
    decode_load.start()
    length_load.start()
    key_load.start()
    x_copy(0).start()
    query_load.start()
    for step in range(1, ranks):
        x_copy(step).start()

    barrier = pltpu.get_barrier_semaphore()

    def greet(peer_group, peer_rank):
        pl.semaphore_signal(
            barrier,
            inc=1,
            device_id={"group": peer_group, "tensor": peer_rank},
            device_id_type=pl.DeviceIdType.MESH,
        )

    for step in range(1, groups):
        greet(group_at(step), rank)
    for step in range(1, ranks):
        greet(group, rank_at(step))

    def slot_copy(step):
        return remote(
            slots.at[rank], slots.at[rank], send_slot.at[step], got_slot.at[rank],
            group, rank_at(step),
        )

    def decode_copy(step):
        peer = group_at(step)
        return remote(
            decode_out.at[peer], decode_all.at[group], send_decode.at[step],
            got_decode.at[group], peer, rank,
        )

    def part_copy(step):
        peer = group_at(step)
        return remote(
            query_part.at[peer], query_in.at[group], send_part.at[step], got_part.at[group],
            peer, rank,
        )

    def query_copy(step):
        return remote(
            query_all.at[rank], query_all.at[rank], send_query.at[step], got_query.at[rank],
            group, rank_at(step),
        )

    def pair_copy(c):
        return remote(
            partial.at[1 - core, c], paired.at[c], send_pair.at[c], got_pair.at[c], group, partner
        )

    def sum_copy(step, c):
        other, peer = chip_at(step)
        return remote(
            chip_sums.at[c, other], incoming.at[c, chip], send_sum.at[c, step],
            got_sum.at[c, chip], group, peer,
        )

    def weight_copy(step, p):
        other, peer = chip_at(step)
        return remote(
            weights.at[p, rank], weights.at[p, rank], send_weight.at[p, step],
            got_weight.at[p, rank], group, peer,
        )

    def on_copy(step, p):
        other, peer = chip_at(step)
        return remote(
            weights.at[p, peer], weights.at[p, peer], send_on.at[p, step],
            got_weight.at[p, peer], group, partner,
        )

    def fresh_copy(step, p):
        peer = rank_at(step)
        return remote(
            fresh_out.at[p, peer], fresh_in.at[p, rank], send_fresh.at[p, step],
            got_fresh.at[p, rank], group, peer,
        )

    def old_copies(step):
        peer = rank_at(step)
        return (
            remote(
                old_out.at[peer], old_in.at[rank], send_old.at[step], got_old.at[rank], group, peer
            ),
            remote(
                old_stat_out.at[peer], old_stat_in.at[rank], send_stat.at[step],
                got_stat.at[rank], group, peer,
            ),
        )

    def cross_copy(step):
        peer = group_at(step)
        return remote(
            cross_out.at[peer], cross_in.at[group], send_cross.at[step], got_cross.at[group],
            peer, rank,
        )

    def arrived(ref, sems, source):
        remote(ref, ref, sems, sems, group, partner).wait_recv()

    slot_load.wait()
    slots[rank] = jnp.broadcast_to(slot_in[0].astype(F32), (PAGE, pages))
    decode_load.wait()
    for g in range(groups):
        for i in range(pieces):
            start = g * depth + i * piece
            fold_wide[g, i * rows : (i + 1) * rows, :] = decode_in[
                :, start : start + piece
            ].astype(F32)
        decode_out[g] = fold_wide[g].astype(BF16)
    pl.semaphore_wait(barrier, groups + ranks - 2)
    for step in range(1, groups):
        decode_copy(step).start()
    for step in range(1, ranks):
        slot_copy(step).start()
    decode_all[group] = decode_out[group]

    spread[...] = jnp.zeros_like(spread)
    lane = iota((1, HEAD_WIDTH), 1)
    sign = jnp.where(lane < half, -1.0, 1.0).astype(F32)
    frequency = jnp.exp(
        jnp.where(lane < half, lane, lane - half).astype(F32)
        * (-2.0 * math.log(rope_theta) / HEAD_WIDTH)
    )
    step_angle = iota((PAGE, HEAD_WIDTH), 0).astype(F32) * frequency
    step_cos, step_sin = jnp.cos(step_angle), jnp.sin(step_angle)
    length_load.wait()
    query_row = iota((query_rows, HEAD_WIDTH), 0)
    position = jnp.zeros((query_rows, HEAD_WIDTH), jnp.int32)
    for b in range(rows):
        position = jnp.where(query_row == b, lengths[b], position)
    query_angle = (position + ranks * span).astype(F32) * frequency
    query_cos, query_sin = jnp.cos(query_angle), jnp.sin(query_angle) * sign

    for step in range(1, ranks):
        source = rank_at(step)
        arrived(slots.at[source], got_slot.at[source], source)

    on_diagonal = iota((pages, pages), 0) == iota((pages, pages), 1)

    def page_tables(t, carry):
        row = jnp.broadcast_to(slots[t][0:1], (pages, pages))
        column = jnp.sum(jnp.where(on_diagonal, row, 0.0), axis=1, keepdims=True)
        place = column - jnp.floor(column * (1.0 / per_owner)) * per_owner
        base = (t * span + offset).astype(F32) + place * PAGE
        angle = base * frequency
        span_t = pl.ds(pl.multiple_of(t * pages, pages), pages)
        page_cos[span_t, :] = jnp.cos(angle)
        page_sin[span_t, :] = jnp.sin(angle)
        return carry

    lax.fori_loop(0, ranks, page_tables, 0)
    widen = (
        (iota((pages, block), 1) >> log2_of(PAGE)) == iota((pages, block), 0)
    ).astype(BF16)
    slot_of[...] = jnp.dot(
        slots[...].reshape(ranks * PAGE, pages).astype(BF16), widen, preferred_element_type=F32
    ).reshape(ranks, PAGE, block)

    def project_queries():
        for step in range(1, groups):
            source = group_at(step)
            arrived(decode_all.at[source], got_decode.at[source], source)
        query_load.wait()
        height, deep = groups * query_rows, groups * FOLD
        m, k = iota((height, deep), 0), iota((height, deep), 1)
        target, row = m >> log2_of(query_rows), m & (query_rows - 1)
        owner, at = k >> log2_of(FOLD), k & (FOLD - 1)
        which, b = at >> log2_of(rows), at & (rows - 1)
        wanted = ((row < rows) & (owner == target) & (b == row)) | (
            (row >= rows) & (owner == row - rows) & (b == target >> log2_of(senders))
        )
        every = decode_all[...].reshape(deep, piece)
        total = jnp.zeros((height, wq.shape[1]), F32)
        for i in range(pieces):
            select = jnp.where(wanted & (which == i), 1.0, 0.0).astype(BF16)
            left = jnp.dot(select, every, preferred_element_type=F32).astype(BF16)
            total = total + jnp.dot(
                left, wq[i * piece : (i + 1) * piece, :], preferred_element_type=F32
            )
        query_part[...] = total.reshape(query_part.shape)
        for step in range(1, groups):
            part_copy(step).start()

    def turn_queries():
        for step in range(1, groups):
            source = group_at(step)
            arrived(query_in.at[source], got_part.at[source], source)
        total = query_part[group]
        for step in range(1, groups):
            total = total + query_in[group_at(step)]
        turned = []
        for h in range(local_heads):
            head = total[:, h * HEAD_WIDTH : (h + 1) * HEAD_WIDTH]
            turned.append(head * query_cos + pltpu.roll(head, half, 1) * query_sin)
        size = local_heads * query_rows
        m, k = iota((size, size), 0), iota((size, size), 1)
        order = (m >> log2_of(local_heads) == k & (query_rows - 1)) & (
            m & (local_heads - 1) == k >> log2_of(query_rows)
        )
        query_all[rank] = jnp.dot(
            jnp.where(order, 1.0, 0.0).astype(BF16),
            stack(turned).astype(BF16),
            preferred_element_type=F32,
        ).astype(BF16)
        for step in range(1, ranks):
            query_copy(step).start()

    def project_keys(t):
        x_copy(t).wait()
        tokens_t = pl.ds(pl.multiple_of(t * block, block), block)
        pages_t = pl.ds(pl.multiple_of(t * pages, pages), pages)
        big_cos = page_cos[pages_t, :].reshape(pages, 1, HEAD_WIDTH)
        big_sin = page_sin[pages_t, :].reshape(pages, 1, HEAD_WIDTH)
        small_cos = step_cos.reshape(1, PAGE, HEAD_WIDTH)
        small_sin = step_sin.reshape(1, PAGE, HEAD_WIDTH)
        cosine = (big_cos * small_cos - big_sin * small_sin).reshape(block, HEAD_WIDTH)
        sine = (big_sin * small_cos + big_cos * small_sin).reshape(block, HEAD_WIDTH) * sign
        wide = 2 * HEAD_WIDTH
        for n in range(kv_width // wide):
            found = jnp.dot(
                x[tokens_t, :], wk[:, n * wide : (n + 1) * wide], preferred_element_type=F32
            )
            for i in range(2):
                head = found[:, i * HEAD_WIDTH : (i + 1) * HEAD_WIDTH]
                start = n * wide + i * HEAD_WIDTH
                keys[tokens_t, start : start + HEAD_WIDTH] = (
                    head * cosine + pltpu.roll(head, half, 1) * sine
                ).astype(BF16)

    key_load.wait()

    def project(t, carry):
        @pl.when(t == 1)
        def _():
            project_queries()

        @pl.when(t == ranks // 2 - 1)
        def _():
            turn_queries()
            value_load.start()
            old_key_load.start()
            old_value_load.start()

        project_keys(t)
        return carry

    lax.fori_loop(0, ranks, project, 0)

    for step in range(1, ranks):
        source = rank_at(step)
        arrived(query_all.at[source], got_query.at[source], source)
    per_tile = FOLD // local_heads
    for r in range(rows + groups):
        for u in range(heads // FOLD):
            members = range(u * per_tile, (u + 1) * per_tile)
            taken = [
                query_all[j].astype(F32)[r * local_heads : (r + 1) * local_heads] for j in members
            ]
            for h in sorted({j * local_heads // per_kv for j in members}):
                spread[
                    r, u * FOLD : (u + 1) * FOLD, h * HEAD_WIDTH : (h + 1) * HEAD_WIDTH
                ] = stack(
                    [
                        value if j * local_heads // per_kv == h else jnp.zeros_like(value)
                        for j, value in zip(members, taken)
                    ]
                ).astype(BF16)

    def add_pair(c):
        arrived(paired.at[c], got_pair.at[c], partner)
        for k in range(chips):
            chip_sums[c, k] = fold(partial[core, c, k] + paired[c, k]).astype(BF16)
        for step in range(1, chips):
            sum_copy(step, c).start()
        own_sums[c] = partial[core, c, chip] + paired[c, chip]

    nt = (((1,), (1,)), ((), ()))

    def score(c, carry):
        for u in range(per_chunk):
            t = c * per_chunk + u
            found = lax.dot_general(
                spread[rows:].reshape(groups * heads, kv_width),
                keys[pl.ds(pl.multiple_of(t * block, block), block), :],
                nt,
                preferred_element_type=F32,
            )
            slot = slot_of[t][0:1]
            kept = found[:heads]
            for o in range(1, groups):
                kept = jnp.where(slot >= o * per_owner, found[o * heads : (o + 1) * heads], kept)
            for j in range(ranks):
                partial[j % 2, c, j // 2, :, u * block : (u + 1) * block] = kept[
                    j * local_heads : (j + 1) * local_heads
                ]
        pair_copy(c).start()

        @pl.when(c > 0)
        def _():
            add_pair(c - 1)

        return carry

    lax.fori_loop(0, CHUNKS, score, 0)

    def attend_old(b):
        found = lax.dot_general(spread[b], old_keys[b], nt, preferred_element_type=F32)
        place = rank * context_dev + iota((1, context_dev), 1)
        found = jnp.where(place < lengths[b], found, masked_score)
        peak = jnp.max(found, axis=-1, keepdims=True)
        exact = jnp.exp2((found - peak) * log_scale)
        amount = jnp.sum(exact, axis=-1, keepdims=True)
        summed = jnp.dot(exact.astype(BF16), old_values[b], preferred_element_type=F32)
        for j in range(ranks):
            h = j * local_heads // per_kv
            old_wide[j, b * local_heads : (b + 1) * local_heads] = summed[
                j * local_heads : (j + 1) * local_heads, h * HEAD_WIDTH : (h + 1) * HEAD_WIDTH
            ]
        return jnp.where(lane == b, peak * log_scale, jnp.where(lane == rows + b, amount, 0.0))

    def softmax(p):
        sums = []
        for c in range(p * per_part, (p + 1) * per_part):
            total = own_sums[c]
            for step in range(1, chips):
                other = chip_at(step)[0]
                arrived(incoming.at[c, other], got_sum.at[c, other], other)
                total = total + unfold(incoming[c, other].astype(F32), local_heads)
            sums.append(total)
        total = beside(sums)
        first = p * per_part * per_chunk
        slot = beside([slot_of[first + u][:local_heads] for u in range(per_part * per_chunk)])
        peak_of = jnp.zeros_like(total)
        for o in range(groups):
            owned = (slot >= o * per_owner) & (slot < (o + 1) * per_owner)
            peak = jnp.max(jnp.where(owned, total, masked_score), axis=-1, keepdims=True)
            peak_of = jnp.where(owned, peak, peak_of)
            peaks[p, o] = jnp.broadcast_to(peak * log_scale, (local_heads, HEAD_WIDTH))
        exact = jnp.exp2((total - peak_of) * log_scale)
        weights[p, rank] = fold(exact).astype(BF16)
        for step in range(1, chips):
            weight_copy(step, p).start()
        on_copy(0, p).start()
        for o in range(groups):
            owned = (slot >= o * per_owner) & (slot < (o + 1) * per_owner)
            amount = jnp.sum(jnp.where(owned, exact, 0.0), axis=-1, keepdims=True)
            totals[p, o] = jnp.broadcast_to(amount, (local_heads, HEAD_WIDTH))

    def pass_on(p):
        for step in range(1, chips):
            peer = chip_at(step)[1]
            arrived(weights.at[p, peer], got_weight.at[p, peer], peer)
            on_copy(step, p).start()

    def mix(p):
        for step in range(chips):
            source = chip_at(step)[0] * 2 + 1 - core
            arrived(weights.at[p, source], got_weight.at[p, source], source)
        width = weights.shape[3]
        for q in range(FOLD // local_heads):
            every = stack(
                [
                    weights[p, j].astype(F32)[q * local_heads : (q + 1) * local_heads]
                    for j in range(ranks)
                ]
            )
            for u in range(width // block):
                start = q * width + u * block
                slot = slot_of[p * (part // block) + start // block][0:1]
                values = every[:, u * block : (u + 1) * block]
                for o in range(groups):
                    owned = (slot >= o * per_owner) & (slot < (o + 1) * per_owner)
                    masked[o * heads : (o + 1) * heads, start : start + block] = jnp.where(
                        owned, values, 0.0
                    ).astype(BF16)
        wide = 2 * HEAD_WIDTH
        for n in range(features // wide):
            mixed[:, n * wide : (n + 1) * wide] = jnp.dot(
                masked[...],
                x[p * part : (p + 1) * part, n * wide : (n + 1) * wide],
                preferred_element_type=F32,
            ).astype(BF16)
        tall = 2 * per_kv
        for n in range(kv_heads // 2):
            left = stack(
                [
                    mixed[o * heads + n * tall : o * heads + (n + 1) * tall, :]
                    for o in range(groups)
                ]
            )
            found = jnp.dot(left, wv[:, n * wide : (n + 1) * wide], preferred_element_type=F32)
            for i in range(tall // local_heads):
                h = i * local_heads // per_kv
                fresh_out[p, n * (tall // local_heads) + i] = stack(
                    [
                        found[
                            o * tall + i * local_heads : o * tall + (i + 1) * local_heads,
                            h * HEAD_WIDTH : (h + 1) * HEAD_WIDTH,
                        ]
                        for o in range(groups)
                    ]
                ).astype(BF16)
        for step in range(1, ranks):
            fresh_copy(step, p).start()

    old_key_load.wait()
    old_value_load.wait()
    about = attend_old(0)
    add_pair(CHUNKS - 1)
    for b in range(1, rows // 2):
        about = about + attend_old(b)
    softmax(0)
    for b in range(rows // 2, rows):
        about = about + attend_old(b)
    pass_on(0)
    for j in range(ranks):
        old_out[j] = old_wide[j].astype(BF16)
        old_stat_out[j] = about[j * local_heads : (j + 1) * local_heads]
    for step in range(1, ranks):
        for copy in old_copies(step):
            copy.start()
    softmax(1)
    value_load.wait()
    mix(0)
    pass_on(1)
    mix(1)

    old_in[rank] = old_out[rank]
    old_stat_in[rank] = old_stat_out[rank]
    for step in range(1, ranks):
        source = rank_at(step)
        arrived(old_in.at[source], got_old.at[source], source)
        arrived(old_stat_in.at[source], got_stat.at[source], source)
    held = []
    for b in range(rows):
        tops = [old_stat_in[r][:, b : b + 1] for r in range(ranks)]
        top = functools.reduce(jnp.maximum, tops)
        numerator, denominator = 0.0, 0.0
        for r in range(ranks):
            factor = jnp.exp2(tops[r] - top)
            numerator = numerator + factor * old_in[r].astype(F32)[
                b * local_heads : (b + 1) * local_heads
            ]
            denominator = denominator + factor * old_stat_in[r][:, rows + b : rows + b + 1]
        held.append((top, numerator, denominator))

    parts = []
    for p in range(PARTS):
        total = fresh_out[p, rank].astype(F32)
        for step in range(1, ranks):
            source = rank_at(step)
            arrived(fresh_in.at[p, source], got_fresh.at[p, source], source)
            total = total + fresh_in[p, source].astype(F32)
        parts.append(total)
    for o in range(groups):
        top = functools.reduce(jnp.maximum, [peaks[p, o] for p in range(PARTS)])
        numerator, denominator = 0.0, 0.0
        for p in range(PARTS):
            factor = jnp.exp2(peaks[p, o] - top)
            numerator = numerator + factor * parts[p][o * local_heads : (o + 1) * local_heads]
            denominator = denominator + factor * totals[p, o]
        cross_out[o, 0] = numerator
        cross_out[o, 1] = jnp.where(lane < half, top, denominator)
    for step in range(1, groups):
        cross_copy(step).start()
    cross_in[group] = cross_out[group]
    for step in range(1, groups):
        source = group_at(step)
        arrived(cross_in.at[source], got_cross.at[source], source)
    for b in range(rows):
        found = [held[b]]
        for source in range(b * senders, (b + 1) * senders):
            stat = cross_in[source, 1]
            found.append((stat[:, 0:1], cross_in[source, 0], stat[:, half : half + 1]))
        top = functools.reduce(jnp.maximum, [item[0] for item in found])
        numerator, denominator = 0.0, 0.0
        for peak, value, amount in found:
            factor = jnp.exp2(peak - top)
            numerator = numerator + factor * value
            denominator = denominator + factor * amount
        out[b] = (numerator / denominator).astype(out.dtype)

    for step in range(1, ranks):
        slot_copy(step).wait_send()
        query_copy(step).wait_send()
        for copy in old_copies(step):
            copy.wait_send()
        for p in range(PARTS):
            fresh_copy(step, p).wait_send()
    for step in range(1, groups):
        decode_copy(step).wait_send()
        part_copy(step).wait_send()
        cross_copy(step).wait_send()
    for c in range(CHUNKS):
        pair_copy(c).wait_send()
        for step in range(1, chips):
            sum_copy(step, c).wait_send()
    for p in range(PARTS):
        for step in range(chips):
            on_copy(step, p).wait_send()
            if step:
                weight_copy(step, p).wait_send()


def per_device(
    prefill_states, key_weight, value_weight, page_slot, decode_states, query_weight,
    cache_keys, cache_values, cached_length,
):
    groups = lax.axis_size("group")
    ranks = lax.axis_size("tensor")
    chips = ranks // 2
    tokens, features = prefill_states.shape
    kv_width = key_weight.shape[1]
    block = tokens // ranks
    pages = block // PAGE
    rows, model = decode_states.shape
    width = query_weight.shape[1]
    local_heads = width // HEAD_WIDTH
    heads = local_heads * ranks
    depth = model // groups
    piece = depth * rows // FOLD
    query_rows = 8
    while query_rows < rows + groups:
        query_rows *= 2
    chunk = tokens // CHUNKS
    part = tokens // PARTS
    dma = pltpu.SemaphoreType.DMA
    vmem = pltpu.VMEM
    hbm = pl.BlockSpec(memory_space=pltpu.HBM)
    result = pl.pallas_call(
        functools.partial(body, groups, ranks),
        in_specs=[hbm] * 9,
        out_specs=pl.BlockSpec(memory_space=pltpu.VMEM),
        out_shape=jax.ShapeDtypeStruct((rows, local_heads, HEAD_WIDTH), BF16),
        scratch_shapes=[
            vmem((tokens, features), BF16),
            vmem((features, kv_width), BF16),
            vmem((features, kv_width), BF16),
            vmem((depth, width), BF16),
            vmem(cache_keys.shape, BF16),
            vmem(cache_values.shape, BF16),
            vmem(page_slot.shape, jnp.int32),
            vmem(decode_states.shape, BF16),
            pltpu.SMEM((rows,), jnp.int32),
            vmem((groups, FOLD, piece), F32),
            vmem((groups, FOLD, piece), BF16),
            vmem((groups, FOLD, piece), BF16),
            vmem((ranks, PAGE, pages), F32),
            vmem((tokens // PAGE, HEAD_WIDTH), F32),
            vmem((tokens // PAGE, HEAD_WIDTH), F32),
            vmem((ranks, PAGE, block), F32),
            vmem((groups, query_rows, width), F32),
            vmem((groups, query_rows, width), F32),
            vmem((ranks, query_rows * local_heads, HEAD_WIDTH), BF16),
            vmem((rows + groups, heads, kv_width), BF16),
            vmem((tokens, kv_width), BF16),
            vmem((2, CHUNKS, chips, local_heads, chunk), F32),
            vmem((CHUNKS, chips, local_heads, chunk), F32),
            vmem((CHUNKS, chips, FOLD, local_heads * chunk // FOLD), BF16),
            vmem((CHUNKS, chips, FOLD, local_heads * chunk // FOLD), BF16),
            vmem((CHUNKS, local_heads, chunk), F32),
            vmem((PARTS, ranks, FOLD, local_heads * part // FOLD), BF16),
            vmem((PARTS, groups, local_heads, HEAD_WIDTH), F32),
            vmem((PARTS, groups, local_heads, HEAD_WIDTH), F32),
            vmem((groups * heads, part), BF16),
            vmem((groups * heads, features), BF16),
            vmem((PARTS, ranks, groups * local_heads, HEAD_WIDTH), BF16),
            vmem((PARTS, ranks, groups * local_heads, HEAD_WIDTH), BF16),
            vmem((ranks, rows * local_heads, HEAD_WIDTH), F32),
            vmem((ranks, rows * local_heads, HEAD_WIDTH), BF16),
            vmem((ranks, rows * local_heads, HEAD_WIDTH), BF16),
            vmem((ranks, local_heads, HEAD_WIDTH), F32),
            vmem((ranks, local_heads, HEAD_WIDTH), F32),
            vmem((groups, 2, local_heads, HEAD_WIDTH), F32),
            vmem((groups, 2, local_heads, HEAD_WIDTH), F32),
            dma((ranks,)), dma((8,)),
            dma((ranks,)), dma((ranks,)), dma((groups,)), dma((groups,)),
            dma((groups,)), dma((groups,)), dma((ranks,)), dma((ranks,)),
            dma((CHUNKS,)), dma((CHUNKS,)), dma((CHUNKS, chips)), dma((CHUNKS, chips)),
            dma((PARTS, chips)), dma((PARTS, chips)), dma((PARTS, ranks)),
            dma((PARTS, ranks)), dma((PARTS, ranks)),
            dma((ranks,)), dma((ranks,)), dma((ranks,)), dma((ranks,)),
            dma((groups,)), dma((groups,)),
        ],
        compiler_params=pltpu.CompilerParams(
            collective_id=0, has_side_effects=True, vmem_limit_bytes=58 * 1024 * 1024
        ),
    )(
        prefill_states, key_weight, value_weight, page_slot, decode_states, query_weight,
        cache_keys, cache_values, cached_length,
    )
    return result.reshape(rows, local_heads * HEAD_WIDTH)


def solution(mesh):
    placed = (
        P("group", "tensor"),
        P("tensor", None),
        P("tensor", None),
        P("group", "tensor", None),
        P("group", None),
        P(None, "tensor"),
        P("group", "tensor", None),
        P("group", "tensor", None),
        P("group"),
    )
    return jax.shard_map(
        per_device, mesh=mesh, in_specs=placed, out_specs=P("group", "tensor"), check_vma=False
    )
```

```python
import functools
import math

import jax
import jax.numpy as jnp
from jax import lax
from jax.experimental import pallas as pl
from jax.experimental.pallas import tpu as pltpu
from jax.sharding import PartitionSpec as P

HEAD_WIDTH = 128
PAGE = 8
FOLD = 16
CHUNKS = 4
PARTS = 2
BOUNDS = (0, 3, 4)
PIECES = 4

rope_theta = 500000.0
masked_score = -1e30
F32, BF16 = jnp.float32, jnp.bfloat16


def log2_of(number):
    power = number.bit_length() - 1
    assert 1 << power == number
    return power


def remote(src, dst, send_sem, recv_sem, group, rank):
    return pltpu.make_async_remote_copy(
        src_ref=src,
        dst_ref=dst,
        send_sem=send_sem,
        recv_sem=recv_sem,
        device_id={"group": group, "tensor": rank},
        device_id_type=pl.DeviceIdType.MESH,
    )


def stack(pieces):
    return pieces[0] if len(pieces) == 1 else jnp.concatenate(pieces, axis=0)


def beside(pieces):
    return pieces[0] if len(pieces) == 1 else jnp.concatenate(pieces, axis=1)


def fold(values):
    count = FOLD // values.shape[0]
    width = values.shape[1] // count
    return stack([values[:, q * width : (q + 1) * width] for q in range(count)])


def unfold(values, height):
    return beside([values[q : q + height] for q in range(0, FOLD, height)])


def iota(shape, axis):
    return lax.broadcasted_iota(jnp.int32, shape, axis)


def body(
    groups, ranks,
    states, key_weight, value_weight, page_slot, decode, query_weight, cache_keys, cache_values,
    cached_length,
    out,
    x, wk, wv, wq, old_keys, old_values, slot_in, decode_in, lengths,
    slots, slot_of, step_cos, step_sin, page_table, far_out, far_in,
    query_all, far_all, spread, keys,
    partial, paired, chip_sums, incoming, own_sums,
    weights_0, weights_1, masked, mixed, fresh_out, fresh_in,
    old_wide, old_out, old_in, old_stat_out, old_stat_in, cross_out, cross_in,
    x_sems, load_sems, wq_sems,
    send_slot, got_slot, send_far, got_far, send_query, got_query, send_near, got_near,
    send_pair, got_pair, send_sum, got_sum, send_weight, got_weight, send_on, got_on,
    send_fresh, got_fresh, send_old, got_old, send_stat, got_stat, send_cross, got_cross,
):
    group, rank = lax.axis_index("group"), lax.axis_index("tensor")
    chips = ranks // 2
    core, chip = lax.rem(rank, 2), rank // 2
    partner = chip * 2 + 1 - core
    own = group * ranks + rank
    tokens, features = x.shape
    block = tokens // ranks
    pages = block // PAGE
    per_owner = pages // groups
    rows, context_dev, kv_width = old_keys.shape
    kv_heads = kv_width // HEAD_WIDTH
    local_heads = out.shape[1]
    heads = local_heads * ranks
    per_kv = heads // kv_heads
    share, span = block // groups, block // rows
    senders = span // share
    offset = lax.rem(group, senders) * share
    query_rows = 2 * rows
    depth = wq.shape[0] // PIECES
    weights = (weights_0, weights_1)
    chunk = tokens // CHUNKS
    per_chunk = chunk // block
    log_scale = math.log2(math.e) / HEAD_WIDTH**0.5
    half = HEAD_WIDTH // 2

    def rank_at(step):
        return lax.rem(rank + step, ranks)

    def group_at(step):
        return lax.rem(group + step, groups)

    def chip_at(step):
        other = lax.rem(chip + step, chips)
        return other, other * 2 + core

    def x_copy(step):
        start = pl.ds(pl.multiple_of(step * block, block), block)
        return pltpu.make_async_copy(states.at[start, :], x.at[start, :], x_sems.at[step])

    def query_load(i):
        span_i = pl.ds(i * depth, depth)
        return pltpu.make_async_copy(query_weight.at[span_i, :], wq.at[span_i, :], wq_sems.at[i])

    def load(source, target, index):
        return pltpu.make_async_copy(source, target, load_sems.at[index])

    key_load = load(key_weight, wk, 0)
    slot_load = load(page_slot, slot_in, 1)
    decode_load = load(decode, decode_in, 2)
    length_load = load(cached_length, lengths, 3)
    value_load = load(value_weight, wv, 4)
    old_key_load = load(cache_keys, old_keys, 5)
    old_value_load = load(cache_values, old_values, 6)

    slot_load.start()
    decode_load.start()
    length_load.start()
    key_load.start()
    x_copy(rank).start()
    for i in range(PIECES):
        query_load(i).start()

    barrier = pltpu.get_barrier_semaphore()

    def greet(peer_group, peer_rank):
        pl.semaphore_signal(
            barrier,
            inc=1,
            device_id={"group": peer_group, "tensor": peer_rank},
            device_id_type=pl.DeviceIdType.MESH,
        )

    for step in range(1, groups):
        greet(group_at(step), rank)
    for step in range(1, ranks):
        greet(group, rank_at(step))

    def slot_copy(step):
        return remote(
            slots.at[rank], slots.at[rank], send_slot, got_slot,
            group, rank_at(step),
        )

    def far_copy(step):
        peer = group_at(step)
        return remote(
            far_out.at[peer], far_in.at[group], send_far, got_far, peer, rank
        )

    def near_copy(step):
        return remote(
            far_all.at[rank], far_all.at[rank], send_near, got_near,
            group, rank_at(step),
        )

    def query_copy(step):
        return remote(
            query_all.at[rank], query_all.at[rank], send_query, got_query,
            group, rank_at(step),
        )

    def pair_copy(c):
        return remote(
            partial.at[1 - core, c], paired.at[c], send_pair, got_pair.at[c], group, partner
        )

    def sum_copy(step, c):
        other, peer = chip_at(step)
        return remote(
            chip_sums.at[c, other], incoming.at[c, chip], send_sum, got_sum.at[c], group, peer,
        )

    def weight_copy(step, p):
        other, peer = chip_at(step)
        return remote(
            weights[p].at[rank], weights[p].at[rank], send_weight.at[p],
            got_weight.at[p], group, peer,
        )

    def on_copy(step, p):
        other, peer = chip_at(step)
        return remote(
            weights[p].at[peer], weights[p].at[peer], send_on.at[p],
            got_on.at[p], group, partner,
        )

    def other_at(step):
        peer = lax.rem(own + step, groups * ranks)
        return peer // ranks, lax.rem(peer, ranks)

    def fresh_copy(step, p):
        peer_group, peer_rank = other_at(step)
        return remote(
            fresh_out.at[p, peer_group * ranks + peer_rank], fresh_in.at[p, own],
            send_fresh.at[p], got_fresh.at[p], peer_group, peer_rank,
        )

    def old_copies(step):
        peer = rank_at(step)
        return (
            remote(
                old_out.at[peer], old_in.at[rank], send_old, got_old, group, peer
            ),
            remote(
                old_stat_out.at[peer], old_stat_in.at[rank], send_stat, got_stat, group, peer,
            ),
        )

    def cross_copy(step):
        peer = group_at(step)
        return remote(
            cross_out.at[peer], cross_in.at[group], send_cross, got_cross,
            peer, rank,
        )

    def arrived(ref, semaphore):
        remote(ref, ref, semaphore, semaphore, group, partner).wait_recv()

    def left(ref, semaphore):
        remote(ref, ref, semaphore, semaphore, group, partner).wait_send()

    other_ranks, other_groups = pl.ds(1, ranks - 1), pl.ds(1, groups - 1)
    other_chips = pl.ds(1, chips - 1)

    lane = iota((1, HEAD_WIDTH), 1)
    sign = jnp.where(lane < half, -1.0, 1.0).astype(F32)
    frequency = jnp.exp(
        jnp.where(lane < half, lane, lane - half).astype(F32)
        * (-2.0 * math.log(rope_theta) / HEAD_WIDTH)
    )
    line = iota((ranks * PAGE, HEAD_WIDTH), 0)
    start = (line >> log2_of(PAGE)) * span + (line & (PAGE - 1)) + offset
    step_angle = start.astype(F32) * frequency
    step_cos[...] = jnp.cos(step_angle).reshape(step_cos.shape)
    step_sin[...] = jnp.sin(step_angle).reshape(step_sin.shape)
    line = iota((pages, HEAD_WIDTH), 0)
    page_angle = ((line & (per_owner - 1)) * PAGE).astype(F32) * frequency
    for i, table in enumerate((jnp.cos(page_angle), jnp.sin(page_angle))):
        high = table.astype(BF16)
        page_table[:, 2 * i * HEAD_WIDTH : (2 * i + 1) * HEAD_WIDTH] = high
        page_table[:, (2 * i + 1) * HEAD_WIDTH : (2 * i + 2) * HEAD_WIDTH] = (
            table - high.astype(F32)
        ).astype(BF16)
    slot_load.wait()
    slots[rank] = jnp.broadcast_to(slot_in[0].astype(F32), (PAGE, pages))
    length_load.wait()
    query_row = iota((query_rows, HEAD_WIDTH), 0)
    position = jnp.zeros((query_rows, HEAD_WIDTH), jnp.int32)
    for b in range(rows):
        position = jnp.where(query_row == b, lengths[b], position)
    query_angle = (position + ranks * span).astype(F32) * frequency
    query_cos, query_sin = jnp.cos(query_angle), jnp.sin(query_angle) * sign
    on_diagonal = iota((pages, pages), 0) == iota((pages, pages), 1)
    page_lane = iota((pages, pages), 1).astype(F32)

    def project_keys(t):
        x_copy(t).wait()
        tokens_t = pl.ds(pl.multiple_of(t * block, block), block)
        row = jnp.broadcast_to(slots[t][0:1], (pages, pages))
        column = jnp.sum(jnp.where(on_diagonal, row, 0.0), axis=1, keepdims=True)
        chosen = jnp.where(page_lane == column, 1.0, 0.0).astype(BF16)
        table = jnp.dot(chosen, page_table[...], preferred_element_type=F32)
        big_cos = (table[:, :HEAD_WIDTH] + table[:, HEAD_WIDTH : 2 * HEAD_WIDTH]).reshape(
            pages, 1, HEAD_WIDTH
        )
        big_sin = (
            table[:, 2 * HEAD_WIDTH : 3 * HEAD_WIDTH] + table[:, 3 * HEAD_WIDTH :]
        ).reshape(pages, 1, HEAD_WIDTH)
        small_cos = step_cos[t].reshape(1, PAGE, HEAD_WIDTH)
        small_sin = step_sin[t].reshape(1, PAGE, HEAD_WIDTH)
        cosine = (big_cos * small_cos - big_sin * small_sin).reshape(block, HEAD_WIDTH)
        sine = (big_sin * small_cos + big_cos * small_sin).reshape(block, HEAD_WIDTH) * sign
        wide = 2 * HEAD_WIDTH
        for n in range(kv_width // wide):
            found = jnp.dot(
                x[tokens_t, :], wk[:, n * wide : (n + 1) * wide], preferred_element_type=F32
            )
            for i in range(2):
                head = found[:, i * HEAD_WIDTH : (i + 1) * HEAD_WIDTH]
                start = n * wide + i * HEAD_WIDTH
                keys[tokens_t, start : start + HEAD_WIDTH] = (
                    head * cosine + pltpu.roll(head, half, 1) * sine
                ).astype(BF16)

    def turn_near():
        arrived(far_in.at[other_groups], got_far)
        far_all[rank] = stack([far_in[o] for o in range(groups)]).astype(BF16)
        for step in range(1, ranks):
            near_copy(step).start()

    def spread_queries():
        arrived(far_all.at[other_ranks], got_near)
        arrived(query_all.at[other_ranks], got_query)
        per_tile = FOLD // local_heads
        for r in range(rows + groups):
            held, at = (query_all, r) if r < rows else (far_all, r - rows)
            for u in range(heads // FOLD):
                members = range(u * per_tile, (u + 1) * per_tile)
                taken = [
                    held[j].astype(F32)[at * local_heads : (at + 1) * local_heads]
                    for j in members
                ]
                for h in sorted({j * local_heads // per_kv for j in members}):
                    spread[
                        r, u * FOLD : (u + 1) * FOLD, h * HEAD_WIDTH : (h + 1) * HEAD_WIDTH
                    ] = stack(
                        [
                            value if j * local_heads // per_kv == h else jnp.zeros_like(value)
                            for j, value in zip(members, taken)
                        ]
                    ).astype(BF16)

    def add_pair(c):
        arrived(paired.at[c], got_pair.at[c])
        for k in range(chips):
            chip_sums[c, k] = fold(partial[core, c, k] + paired[c, k]).astype(BF16)
        for step in range(1, chips):
            sum_copy(step, c).start()
        own_sums[c] = partial[core, c, chip] + paired[c, chip]

    nt = (((1,), (1,)), ((), ()))

    def score(first, c, carry):
        for u in range(per_chunk):
            t = c * per_chunk + u
            found = lax.dot_general(
                spread[rows:].reshape(groups * heads, kv_width),
                keys[pl.ds(pl.multiple_of(t * block, block), block), :],
                nt,
                preferred_element_type=F32,
            )
            slot = slot_of[t][0:1]
            kept = found[:heads]
            for o in range(1, groups):
                kept = jnp.where(slot >= o * per_owner, found[o * heads : (o + 1) * heads], kept)
            for j in range(ranks):
                partial[j % 2, c, j // 2, :, u * block : (u + 1) * block] = kept[
                    j * local_heads : (j + 1) * local_heads
                ]
        pair_copy(c).start()

        @pl.when(c > first)
        def _():
            add_pair(c - 1)

        return carry

    key_load.wait()
    project_keys(rank)
    decode_load.wait()
    turns = depth // min(depth, 1024)

    def add_piece(i, total):
        span_i = pl.ds(pl.multiple_of(i * (depth // turns), depth // turns), depth // turns)
        return total + jnp.dot(
            decode_in[:, span_i], wq[span_i, :], preferred_element_type=F32
        )

    total = jnp.zeros((rows, wq.shape[1]), F32)
    for i in range(PIECES):
        query_load(i).wait()
        total = lax.fori_loop(i * turns, (i + 1) * turns, add_piece, total)
        if i == PIECES // 2 - 1:
            pl.semaphore_wait(barrier, groups + ranks - 2)
            for step in range(1, ranks):
                slot_copy(step).start()
            for step in range(1, ranks):
                x_copy(rank_at(step)).start()
    total = stack([total, total])
    turned = []
    for h in range(local_heads):
        head = total[:, h * HEAD_WIDTH : (h + 1) * HEAD_WIDTH]
        turned.append(head * query_cos + pltpu.roll(head, half, 1) * query_sin)
    size = local_heads * query_rows
    m, k = iota((size, size), 0), iota((size, size), 1)
    order = (m >> log2_of(local_heads) == k & (query_rows - 1)) & (
        m & (local_heads - 1) == k >> log2_of(query_rows)
    )
    arranged = jnp.dot(
        jnp.where(order, 1.0, 0.0).astype(BF16),
        stack(turned).astype(BF16),
        preferred_element_type=F32,
    )
    for g in range(groups):
        at = (rows + g // senders) * local_heads
        far_out[g] = arranged[at : at + local_heads]
    for step in range(1, groups):
        far_copy(step).start()
    query_all[rank] = arranged[: rows * local_heads].astype(BF16)
    for step in range(1, ranks):
        query_copy(step).start()
    far_in[group] = far_out[group]
    value_load.start()
    old_key_load.start()
    old_value_load.start()
    spread[...] = jnp.zeros_like(spread)
    arrived(slots.at[other_ranks], got_slot)
    widen = (
        (iota((pages, block), 1) >> log2_of(PAGE)) == iota((pages, block), 0)
    ).astype(BF16)
    slot_of[...] = jnp.dot(
        slots[...].reshape(ranks * PAGE, pages).astype(BF16), widen, preferred_element_type=F32
    ).reshape(ranks, PAGE, block)

    near_tick, score_tick = 3 * ranks // 8, ranks - 3

    def scored(tick):
        ready = jnp.where(tick == ranks - 1, CHUNKS, tick // per_chunk)
        return jnp.where(tick < score_tick, 0, ready)

    def project(tick, carry):
        @pl.when(tick == near_tick)
        def _():
            turn_near()

        project_keys(jnp.where(tick - 1 < rank, tick - 1, tick))
        before, first, last = scored(tick - 2), scored(tick - 1), scored(tick)

        @pl.when(first > before)
        def _():
            add_pair(first - 1)

        @pl.when(tick == score_tick)
        def _():
            spread_queries()

        lax.fori_loop(first, last, functools.partial(score, first), 0)
        return carry

    lax.fori_loop(1, ranks, project, 0)

    def attend_old(b):
        found = lax.dot_general(spread[b], old_keys[b], nt, preferred_element_type=F32)
        place = rank * context_dev + iota((1, context_dev), 1)
        found = jnp.where(place < lengths[b], found, masked_score)
        peak = jnp.max(found, axis=-1, keepdims=True)
        exact = jnp.exp2((found - peak) * log_scale)
        amount = jnp.sum(exact, axis=-1, keepdims=True)
        summed = jnp.dot(exact.astype(BF16), old_values[b], preferred_element_type=F32)
        for j in range(ranks):
            h = j * local_heads // per_kv
            old_wide[j, b * local_heads : (b + 1) * local_heads] = summed[
                j * local_heads : (j + 1) * local_heads, h * HEAD_WIDTH : (h + 1) * HEAD_WIDTH
            ]
        return jnp.where(lane == b, peak * log_scale, jnp.where(lane == rows + b, amount, 0.0))

    def softmax(p):
        sums = []
        for c in range(BOUNDS[p], BOUNDS[p + 1]):
            total = own_sums[c]
            arrived(incoming.at[c, other_chips], got_sum.at[c])
            for step in range(1, chips):
                other = chip_at(step)[0]
                total = total + unfold(incoming[c, other].astype(F32), local_heads)
            sums.append(total)
        total = beside(sums)
        slot = beside(
            [
                slot_of[t][:local_heads]
                for t in range(BOUNDS[p] * per_chunk, BOUNDS[p + 1] * per_chunk)
            ]
        )
        peak_of, peaks = jnp.zeros_like(total), []
        for o in range(groups):
            owned = (slot >= o * per_owner) & (slot < (o + 1) * per_owner)
            peak = jnp.max(jnp.where(owned, total, masked_score), axis=-1, keepdims=True)
            peak_of = jnp.where(owned, peak, peak_of)
            peaks.append(peak * log_scale)
        exact = jnp.exp2((total - peak_of) * log_scale)
        weights[p][rank] = fold(exact).astype(BF16)
        for step in range(1, chips):
            weight_copy(step, p).start()
        on_copy(0, p).start()
        for o in range(groups):
            owned = (slot >= o * per_owner) & (slot < (o + 1) * per_owner)
            amount = jnp.sum(jnp.where(owned, exact, 0.0), axis=-1, keepdims=True)
            cross_out[o, p] = jnp.where(lane < half, peaks[o], amount)

    def pass_on(p):
        arrived(weights[p].at[other_chips], got_weight.at[p])
        for step in range(1, chips):
            on_copy(step, p).start()

    def mix(p):
        arrived(weights[p].at[pl.ds(0, chips)], got_on.at[p])
        width = weights[p].shape[2]
        base = BOUNDS[p] * chunk
        part = (BOUNDS[p + 1] - BOUNDS[p]) * chunk
        for q in range(FOLD // local_heads):
            every = stack(
                [
                    weights[p][j].astype(F32)[q * local_heads : (q + 1) * local_heads]
                    for j in range(ranks)
                ]
            )
            for u in range(width // block):
                start = q * width + u * block
                slot = slot_of[(base + start) // block][0:1]
                values = every[:, u * block : (u + 1) * block]
                for o in range(groups):
                    owned = (slot >= o * per_owner) & (slot < (o + 1) * per_owner)
                    masked[o * heads : (o + 1) * heads, start : start + block] = jnp.where(
                        owned, values, 0.0
                    ).astype(BF16)
        wide = 2 * HEAD_WIDTH
        for n in range(features // wide):
            mixed[:, n * wide : (n + 1) * wide] = jnp.dot(
                masked[:, :part],
                x[base : base + part, n * wide : (n + 1) * wide],
                preferred_element_type=F32,
            ).astype(BF16)
        tall = 2 * per_kv
        for n in range(kv_heads // 2):
            left = stack(
                [
                    mixed[o * heads + n * tall : o * heads + (n + 1) * tall, :]
                    for o in range(groups)
                ]
            )
            found = jnp.dot(left, wv[:, n * wide : (n + 1) * wide], preferred_element_type=F32)
            for i in range(tall // local_heads):
                h = i * local_heads // per_kv
                for o in range(groups):
                    at = o * tall + i * local_heads
                    fresh_out[p, o * ranks + n * (tall // local_heads) + i] = found[
                        at : at + local_heads, h * HEAD_WIDTH : (h + 1) * HEAD_WIDTH
                    ]

        def start(step, carry):
            fresh_copy(step, p).start()
            return carry

        lax.fori_loop(1, groups * ranks, start, 0)
        fresh_in[p, own] = fresh_out[p, own]

    old_key_load.wait()
    old_value_load.wait()
    about = attend_old(0)
    add_pair(CHUNKS - 1)
    for b in range(1, rows // 2):
        about = about + attend_old(b)
    softmax(0)
    for b in range(rows // 2, rows):
        about = about + attend_old(b)
    softmax(1)
    for step in range(1, groups):
        cross_copy(step).start()
    cross_in[group] = cross_out[group]
    for j in range(ranks):
        old_out[j] = old_wide[j].astype(BF16)
        old_stat_out[j] = about[j * local_heads : (j + 1) * local_heads]
    pass_on(0)
    value_load.wait()
    mix(0)
    pass_on(1)
    for step in range(1, ranks):
        for copy in old_copies(step):
            copy.start()
    mix(1)

    old_in[rank] = old_out[rank]
    old_stat_in[rank] = old_stat_out[rank]
    arrived(old_in.at[other_ranks], got_old)
    arrived(old_stat_in.at[other_ranks], got_stat)
    held = []
    for b in range(rows):
        tops = [old_stat_in[r][:, b : b + 1] for r in range(ranks)]
        top = functools.reduce(jnp.maximum, tops)
        numerator, denominator = 0.0, 0.0
        for r in range(ranks):
            factor = jnp.exp2(tops[r] - top)
            numerator = numerator + factor * old_in[r].astype(F32)[
                b * local_heads : (b + 1) * local_heads
            ]
            denominator = denominator + factor * old_stat_in[r][:, rows + b : rows + b + 1]
        held.append((top, numerator, denominator))

    arrived(cross_in.at[other_groups], got_cross)
    found = [[item] for item in held]
    for p in range(PARTS):
        arrived(fresh_in.at[p, pl.ds(1, groups * ranks - 1)], got_fresh.at[p])
        for source in range(groups):
            stat = cross_in[source, p]
            total = jnp.sum(fresh_in[p, source * ranks : (source + 1) * ranks], axis=0)
            found[source // senders].append((stat[:, 0:1], total, stat[:, half : half + 1]))
    for b in range(rows):
        top = functools.reduce(jnp.maximum, [item[0] for item in found[b]])
        numerator, denominator = 0.0, 0.0
        for peak, value, amount in found[b]:
            factor = jnp.exp2(peak - top)
            numerator = numerator + factor * value
            denominator = denominator + factor * amount
        out[b] = (numerator / denominator).astype(out.dtype)

    left(slots.at[other_ranks], send_slot)
    left(query_all.at[other_ranks], send_query)
    left(far_all.at[other_ranks], send_near)
    left(far_in.at[other_groups], send_far)
    left(old_in.at[other_ranks], send_old)
    left(old_stat_in.at[other_ranks], send_stat)
    left(cross_in.at[other_groups], send_cross)
    left(paired, send_pair)
    left(incoming.at[:, other_chips], send_sum)
    for p in range(PARTS):
        left(weights[p].at[other_chips], send_weight.at[p])
        left(weights[p].at[pl.ds(0, chips)], send_on.at[p])
        left(fresh_in.at[p, pl.ds(1, groups * ranks - 1)], send_fresh.at[p])


def per_device(
    prefill_states, key_weight, value_weight, page_slot, decode_states, query_weight,
    cache_keys, cache_values, cached_length,
):
    groups = lax.axis_size("group")
    ranks = lax.axis_size("tensor")
    chips = ranks // 2
    tokens, features = prefill_states.shape
    kv_width = key_weight.shape[1]
    block = tokens // ranks
    pages = block // PAGE
    rows, model = decode_states.shape
    width = query_weight.shape[1]
    local_heads = width // HEAD_WIDTH
    heads = local_heads * ranks
    chunk = tokens // CHUNKS
    widths = [
        local_heads * chunk * (BOUNDS[p + 1] - BOUNDS[p]) // FOLD for p in range(PARTS)
    ]
    longest = chunk * max(BOUNDS[p + 1] - BOUNDS[p] for p in range(PARTS))
    dma = pltpu.SemaphoreType.DMA
    vmem = pltpu.VMEM
    hbm = pl.BlockSpec(memory_space=pltpu.HBM)
    result = pl.pallas_call(
        functools.partial(body, groups, ranks),
        in_specs=[hbm] * 9,
        out_specs=pl.BlockSpec(memory_space=pltpu.VMEM),
        out_shape=jax.ShapeDtypeStruct((rows, local_heads, HEAD_WIDTH), BF16),
        scratch_shapes=[
            vmem((tokens, features), BF16),
            vmem((features, kv_width), BF16),
            vmem((features, kv_width), BF16),
            vmem(query_weight.shape, BF16),
            vmem(cache_keys.shape, BF16),
            vmem(cache_values.shape, BF16),
            vmem(page_slot.shape, jnp.int32),
            vmem(decode_states.shape, BF16),
            pltpu.SMEM((rows,), jnp.int32),
            vmem((ranks, PAGE, pages), F32),
            vmem((ranks, PAGE, block), F32),
            vmem((ranks, PAGE, HEAD_WIDTH), F32),
            vmem((ranks, PAGE, HEAD_WIDTH), F32),
            vmem((pages, 4 * HEAD_WIDTH), BF16),
            vmem((groups, local_heads, HEAD_WIDTH), F32),
            vmem((groups, local_heads, HEAD_WIDTH), F32),
            vmem((ranks, rows * local_heads, HEAD_WIDTH), BF16),
            vmem((ranks, groups * local_heads, HEAD_WIDTH), BF16),
            vmem((rows + groups, heads, kv_width), BF16),
            vmem((tokens, kv_width), BF16),
            vmem((2, CHUNKS, chips, local_heads, chunk), F32),
            vmem((CHUNKS, chips, local_heads, chunk), F32),
            vmem((CHUNKS, chips, FOLD, local_heads * chunk // FOLD), BF16),
            vmem((CHUNKS, chips, FOLD, local_heads * chunk // FOLD), BF16),
            vmem((CHUNKS, local_heads, chunk), F32),
            vmem((ranks, FOLD, widths[0]), BF16),
            vmem((ranks, FOLD, widths[1]), BF16),
            vmem((groups * heads, longest), BF16),
            vmem((groups * heads, features), BF16),
            vmem((PARTS, groups * ranks, local_heads, HEAD_WIDTH), F32),
            vmem((PARTS, groups * ranks, local_heads, HEAD_WIDTH), F32),
            vmem((ranks, rows * local_heads, HEAD_WIDTH), F32),
            vmem((ranks, rows * local_heads, HEAD_WIDTH), BF16),
            vmem((ranks, rows * local_heads, HEAD_WIDTH), BF16),
            vmem((ranks, local_heads, HEAD_WIDTH), F32),
            vmem((ranks, local_heads, HEAD_WIDTH), F32),
            vmem((groups, PARTS, local_heads, HEAD_WIDTH), F32),
            vmem((groups, PARTS, local_heads, HEAD_WIDTH), F32),
            dma((ranks,)), dma((7,)), dma((PIECES,)),
            dma, dma, dma, dma, dma, dma, dma, dma,
            dma, dma((CHUNKS,)), dma, dma((CHUNKS,)),
            dma((PARTS,)), dma((PARTS,)), dma((PARTS,)), dma((PARTS,)),
            dma((PARTS,)), dma((PARTS,)), dma, dma, dma, dma, dma, dma,
        ],
        compiler_params=pltpu.CompilerParams(
            collective_id=0, has_side_effects=True, vmem_limit_bytes=58 * 1024 * 1024
        ),
    )(
        prefill_states, key_weight, value_weight, page_slot, decode_states, query_weight,
        cache_keys, cache_values, cached_length,
    )
    return result.reshape(rows, local_heads * HEAD_WIDTH)


def solution(mesh):
    placed = (
        P("group", "tensor"),
        P("tensor", None),
        P("tensor", None),
        P("group", "tensor", None),
        P("group", None),
        P(None, "tensor"),
        P("group", "tensor", None),
        P("group", "tensor", None),
        P("group"),
    )
    return jax.shard_map(
        per_device, mesh=mesh, in_specs=placed, out_specs=P("group", "tensor"), check_vma=False
    )
```

```python
import functools
import math

import jax
import jax.numpy as jnp
from jax import lax
from jax.experimental import pallas as pl
from jax.experimental.pallas import tpu as pltpu
from jax.sharding import PartitionSpec as P

HEAD_WIDTH = 128
PAGE = 8
FOLD = 16
CHUNKS = 4
PARTS = 2
BOUNDS = (0, 3, 4)
PIECES = 4

rope_theta = 500000.0
masked_score = -1e30
F32, BF16 = jnp.float32, jnp.bfloat16


def log2_of(number):
    power = number.bit_length() - 1
    assert 1 << power == number
    return power


def remote(src, dst, send_sem, recv_sem, group, rank):
    return pltpu.make_async_remote_copy(
        src_ref=src,
        dst_ref=dst,
        send_sem=send_sem,
        recv_sem=recv_sem,
        device_id={"group": group, "tensor": rank},
        device_id_type=pl.DeviceIdType.MESH,
    )


def stack(pieces):
    return pieces[0] if len(pieces) == 1 else jnp.concatenate(pieces, axis=0)


def beside(pieces):
    return pieces[0] if len(pieces) == 1 else jnp.concatenate(pieces, axis=1)


def fold(values):
    count = FOLD // values.shape[0]
    width = values.shape[1] // count
    return stack([values[:, q * width : (q + 1) * width] for q in range(count)])


def unfold(values, height):
    return beside([values[q : q + height] for q in range(0, FOLD, height)])


def iota(shape, axis):
    return lax.broadcasted_iota(jnp.int32, shape, axis)


def body(
    groups, ranks,
    states, key_weight, value_weight, page_slot, decode, query_weight, cache_keys, cache_values,
    cached_length,
    out,
    x, wk, wv, wq, old_keys, old_values, slot_in, decode_in, lengths,
    slots, slot_of, step_cos, step_sin, page_table, far_out, far_in,
    query_all, far_all, spread, keys,
    partial, paired, chip_sums, incoming, own_sums,
    weights_0, weights_1, masked, mixed, fresh_wide, fresh_out, fresh_in,
    old_wide, old_out, old_in, old_stat_out, old_stat_in, cross_out, cross_in,
    x_sems, load_sems, wq_sems,
    send_slot, got_slot, send_far, got_far, send_query, got_query, send_near, got_near,
    send_pair, got_pair, send_sum, got_sum, send_weight, got_weight, send_on, got_on,
    send_fresh, got_fresh, send_old, got_old, send_stat, got_stat, send_cross, got_cross,
):
    group, rank = lax.axis_index("group"), lax.axis_index("tensor")
    chips = ranks // 2
    core, chip = lax.rem(rank, 2), rank // 2
    partner = chip * 2 + 1 - core
    own = group * ranks + rank
    tokens, features = x.shape
    block = tokens // ranks
    pages = block // PAGE
    per_owner = pages // groups
    rows, context_dev, kv_width = old_keys.shape
    kv_heads = kv_width // HEAD_WIDTH
    local_heads = out.shape[1]
    heads = local_heads * ranks
    per_kv = heads // kv_heads
    share, span = block // groups, block // rows
    senders = span // share
    offset = lax.rem(group, senders) * share
    query_rows = 2 * rows
    depth = wq.shape[0] // PIECES
    weights = (weights_0, weights_1)
    chunk = tokens // CHUNKS
    per_chunk = chunk // block
    two_heads = 2 * HEAD_WIDTH
    assert FOLD == 2 * per_kv
    log_scale = math.log2(math.e) / HEAD_WIDTH**0.5
    half = HEAD_WIDTH // 2

    def rank_at(step):
        return lax.rem(rank + step, ranks)

    def group_at(step):
        return lax.rem(group + step, groups)

    def chip_at(step):
        other = lax.rem(chip + step, chips)
        return other, other * 2 + core

    def x_copy(step):
        start = pl.ds(pl.multiple_of(step * block, block), block)
        return pltpu.make_async_copy(states.at[start, :], x.at[start, :], x_sems.at[step])

    def query_load(i):
        span_i = pl.ds(i * depth, depth)
        return pltpu.make_async_copy(query_weight.at[span_i, :], wq.at[span_i, :], wq_sems.at[i])

    def load(source, target, index):
        return pltpu.make_async_copy(source, target, load_sems.at[index])

    key_load = load(key_weight, wk, 0)
    slot_load = load(page_slot, slot_in, 1)
    decode_load = load(decode, decode_in, 2)
    length_load = load(cached_length, lengths, 3)
    value_load = load(value_weight, wv, 4)
    old_key_load = load(cache_keys, old_keys, 5)
    old_value_load = load(cache_values, old_values, 6)

    slot_load.start()
    decode_load.start()
    length_load.start()
    key_load.start()
    x_copy(rank).start()
    query_load(0).start()

    barrier = pltpu.get_barrier_semaphore()

    def greet(peer_group, peer_rank):
        pl.semaphore_signal(
            barrier,
            inc=1,
            device_id={"group": peer_group, "tensor": peer_rank},
            device_id_type=pl.DeviceIdType.MESH,
        )

    for step in range(1, groups):
        greet(group_at(step), rank)
    for step in range(1, ranks):
        greet(group, rank_at(step))

    def slot_copy(step):
        return remote(
            slots.at[rank], slots.at[rank], send_slot, got_slot,
            group, rank_at(step),
        )

    def far_copy(step):
        peer = group_at(step)
        return remote(
            far_out.at[peer], far_in.at[group], send_far, got_far, peer, rank
        )

    def near_copy(step):
        return remote(
            far_all.at[rank], far_all.at[rank], send_near, got_near,
            group, rank_at(step),
        )

    def query_copy(step):
        return remote(
            query_all.at[rank], query_all.at[rank], send_query, got_query,
            group, rank_at(step),
        )

    def pair_copy(c):
        return remote(
            partial.at[1 - core, c], paired.at[c], send_pair, got_pair.at[c], group, partner
        )

    def sum_copy(step, c):
        other, peer = chip_at(step)
        return remote(
            chip_sums.at[c, other], incoming.at[c, chip], send_sum, got_sum.at[c], group, peer,
        )

    def weight_copy(step, p):
        other, peer = chip_at(step)
        return remote(
            weights[p].at[rank], weights[p].at[rank], send_weight.at[p],
            got_weight.at[p], group, peer,
        )

    def on_copy(step, p):
        other, peer = chip_at(step)
        return remote(
            weights[p].at[peer], weights[p].at[peer], send_on.at[p],
            got_on.at[p], group, partner,
        )

    def other_at(step):
        peer = lax.rem(own + step, groups * ranks)
        return peer // ranks, lax.rem(peer, ranks)

    def fresh_copy(step):
        peer_group, peer_rank = other_at(step)
        return remote(
            fresh_out.at[peer_group * ranks + peer_rank], fresh_in.at[own],
            send_fresh, got_fresh, peer_group, peer_rank,
        )

    def old_copies(step):
        peer = rank_at(step)
        return (
            remote(
                old_out.at[peer], old_in.at[rank], send_old, got_old, group, peer
            ),
            remote(
                old_stat_out.at[peer], old_stat_in.at[rank], send_stat, got_stat, group, peer,
            ),
        )

    def cross_copy(step):
        peer = group_at(step)
        return remote(
            cross_out.at[peer], cross_in.at[group], send_cross, got_cross,
            peer, rank,
        )

    def arrived(ref, semaphore):
        remote(ref, ref, semaphore, semaphore, group, partner).wait_recv()

    def left(ref, semaphore):
        remote(ref, ref, semaphore, semaphore, group, partner).wait_send()

    other_ranks, other_groups = pl.ds(1, ranks - 1), pl.ds(1, groups - 1)
    other_chips = pl.ds(1, chips - 1)

    lane = iota((1, HEAD_WIDTH), 1)
    sign = jnp.where(lane < half, -1.0, 1.0).astype(F32)
    frequency = jnp.exp(
        jnp.where(lane < half, lane, lane - half).astype(F32)
        * (-2.0 * math.log(rope_theta) / HEAD_WIDTH)
    )
    line = iota((ranks * PAGE, HEAD_WIDTH), 0)
    start = (line >> log2_of(PAGE)) * span + (line & (PAGE - 1)) + offset
    step_angle = start.astype(F32) * frequency
    step_cos[...] = jnp.cos(step_angle).reshape(step_cos.shape)
    step_sin[...] = jnp.sin(step_angle).reshape(step_sin.shape)
    line = iota((pages, HEAD_WIDTH), 0)
    page_angle = ((line & (per_owner - 1)) * PAGE).astype(F32) * frequency
    for i, table in enumerate((jnp.cos(page_angle), jnp.sin(page_angle))):
        high = table.astype(BF16)
        page_table[:, 2 * i * HEAD_WIDTH : (2 * i + 1) * HEAD_WIDTH] = high
        page_table[:, (2 * i + 1) * HEAD_WIDTH : (2 * i + 2) * HEAD_WIDTH] = (
            table - high.astype(F32)
        ).astype(BF16)
    slot_load.wait()
    slots[rank] = jnp.broadcast_to(slot_in[0].astype(F32), (PAGE, pages))
    length_load.wait()
    query_row = iota((query_rows, HEAD_WIDTH), 0)
    position = jnp.zeros((query_rows, HEAD_WIDTH), jnp.int32)
    for b in range(rows):
        position = jnp.where(query_row == b, lengths[b], position)
    query_angle = (position + ranks * span).astype(F32) * frequency
    query_cos, query_sin = jnp.cos(query_angle), jnp.sin(query_angle) * sign
    on_diagonal = iota((pages, pages), 0) == iota((pages, pages), 1)
    page_lane = iota((pages, pages), 1).astype(F32)

    def project_keys(t):
        tokens_t = pl.ds(pl.multiple_of(t * block, block), block)
        row = jnp.broadcast_to(slots[t][0:1], (pages, pages))
        column = jnp.sum(jnp.where(on_diagonal, row, 0.0), axis=1, keepdims=True)
        chosen = jnp.where(page_lane == column, 1.0, 0.0).astype(BF16)
        table = jnp.dot(chosen, page_table[...], preferred_element_type=F32)
        big_cos = (table[:, :HEAD_WIDTH] + table[:, HEAD_WIDTH : 2 * HEAD_WIDTH]).reshape(
            pages, 1, HEAD_WIDTH
        )
        big_sin = (
            table[:, 2 * HEAD_WIDTH : 3 * HEAD_WIDTH] + table[:, 3 * HEAD_WIDTH :]
        ).reshape(pages, 1, HEAD_WIDTH)
        small_cos = step_cos[t].reshape(1, PAGE, HEAD_WIDTH)
        small_sin = step_sin[t].reshape(1, PAGE, HEAD_WIDTH)
        cosine = (big_cos * small_cos - big_sin * small_sin).reshape(block, HEAD_WIDTH)
        sine = (big_sin * small_cos + big_cos * small_sin).reshape(block, HEAD_WIDTH) * sign
        wide = 2 * HEAD_WIDTH
        for n in range(kv_width // wide):
            found = jnp.dot(
                x[tokens_t, :], wk[:, n * wide : (n + 1) * wide], preferred_element_type=F32
            )
            for i in range(2):
                head = found[:, i * HEAD_WIDTH : (i + 1) * HEAD_WIDTH]
                start = n * wide + i * HEAD_WIDTH
                keys[tokens_t, start : start + HEAD_WIDTH] = (
                    head * cosine + pltpu.roll(head, half, 1) * sine
                ).astype(BF16)

    def turn_near():
        arrived(far_in.at[other_groups], got_far)
        far_all[rank] = stack([far_in[o] for o in range(groups)]).astype(BF16)
        for step in range(1, ranks):
            near_copy(step).start()

    def spread_queries():
        arrived(far_all.at[other_ranks], got_near)
        arrived(query_all.at[other_ranks], got_query)
        per_tile = FOLD // local_heads
        for r in range(rows + groups):
            held, at = (query_all, r) if r < rows else (far_all, r - rows)
            for u in range(heads // FOLD):
                members = range(u * per_tile, (u + 1) * per_tile)
                taken = [
                    held[j].astype(F32)[at * local_heads : (at + 1) * local_heads]
                    for j in members
                ]
                for h in sorted({j * local_heads // per_kv for j in members}):
                    first = h * HEAD_WIDTH - u * two_heads
                    spread[u, r, :, first : first + HEAD_WIDTH] = stack(
                        [
                            value if j * local_heads // per_kv == h else jnp.zeros_like(value)
                            for j, value in zip(members, taken)
                        ]
                    ).astype(BF16)

    def add_pair(c):
        arrived(paired.at[c], got_pair.at[c])
        for k in range(chips):
            chip_sums[c, k] = fold(partial[core, c, k] + paired[c, k]).astype(BF16)
        for step in range(1, chips):
            sum_copy(step, c).start()
        own_sums[c] = partial[core, c, chip] + paired[c, chip]

    nt = (((1,), (1,)), ((), ()))

    def score(first, c, carry):
        for u in range(per_chunk):
            t = c * per_chunk + u
            slot = slot_of[t][0:1]
            for n in range(heads // FOLD):
                found = lax.dot_general(
                    spread[n, rows:].reshape(groups * FOLD, two_heads),
                    keys[
                        pl.ds(pl.multiple_of(t * block, block), block),
                        n * two_heads : (n + 1) * two_heads,
                    ],
                    nt,
                    preferred_element_type=F32,
                )
                kept = found[:FOLD]
                for o in range(1, groups):
                    kept = jnp.where(
                        slot >= o * per_owner, found[o * FOLD : (o + 1) * FOLD], kept
                    )
                for i in range(FOLD // local_heads):
                    j = n * (FOLD // local_heads) + i
                    partial[j % 2, c, j // 2, :, u * block : (u + 1) * block] = kept[
                        i * local_heads : (i + 1) * local_heads
                    ]
        pair_copy(c).start()

        @pl.when(c > first)
        def _():
            add_pair(c - 1)

        return carry

    def block_at(tick):
        return jnp.where(tick - 1 < rank, tick - 1, tick)

    key_load.wait()
    x_copy(rank).wait()
    for i in range(1, PIECES):
        query_load(i).start()
    project_keys(rank)
    pl.semaphore_wait(barrier, groups + ranks - 2)
    for step in range(1, ranks):
        slot_copy(step).start()
    decode_load.wait()
    turns = depth // min(depth, 1024)

    def add_piece(i, total):
        span_i = pl.ds(pl.multiple_of(i * (depth // turns), depth // turns), depth // turns)
        return total + jnp.dot(
            decode_in[:, span_i], wq[span_i, :], preferred_element_type=F32
        )

    total = jnp.zeros((rows, wq.shape[1]), F32)
    for i in range(PIECES):
        query_load(i).wait()
        total = lax.fori_loop(i * turns, (i + 1) * turns, add_piece, total)
        if i == PIECES - 2:
            for tick in range(1, ranks):
                x_copy(block_at(tick)).start()
    total = stack([total, total])
    turned = []
    for h in range(local_heads):
        head = total[:, h * HEAD_WIDTH : (h + 1) * HEAD_WIDTH]
        turned.append(head * query_cos + pltpu.roll(head, half, 1) * query_sin)
    size = local_heads * query_rows
    m, k = iota((size, size), 0), iota((size, size), 1)
    order = (m >> log2_of(local_heads) == k & (query_rows - 1)) & (
        m & (local_heads - 1) == k >> log2_of(query_rows)
    )
    arranged = jnp.dot(
        jnp.where(order, 1.0, 0.0).astype(BF16),
        stack(turned).astype(BF16),
        preferred_element_type=F32,
    )
    for g in range(groups):
        at = (rows + g // senders) * local_heads
        far_out[g] = arranged[at : at + local_heads]
    for step in range(1, groups):
        far_copy(step).start()
    query_all[rank] = arranged[: rows * local_heads].astype(BF16)
    for step in range(1, ranks):
        query_copy(step).start()
    far_in[group] = far_out[group]
    value_load.start()
    old_key_load.start()
    old_value_load.start()
    arrived(slots.at[other_ranks], got_slot)
    widen = (
        (iota((pages, block), 1) >> log2_of(PAGE)) == iota((pages, block), 0)
    ).astype(BF16)
    slot_of[...] = jnp.dot(
        slots[...].reshape(ranks * PAGE, pages).astype(BF16), widen, preferred_element_type=F32
    ).reshape(ranks, PAGE, block)

    near_tick, score_tick = 3 * ranks // 8, ranks - 3

    def scored(tick):
        ready = jnp.where(tick == ranks - 1, CHUNKS, tick // per_chunk)
        return jnp.where(tick < score_tick, 0, ready)

    def project(tick, carry):
        @pl.when(tick == near_tick)
        def _():
            turn_near()

        t = block_at(tick)
        x_copy(t).wait()
        project_keys(t)
        before, first, last = scored(tick - 2), scored(tick - 1), scored(tick)

        @pl.when(first > before)
        def _():
            add_pair(first - 1)

        @pl.when(tick == score_tick)
        def _():
            spread_queries()

        lax.fori_loop(first, last, functools.partial(score, first), 0)
        return carry

    lax.fori_loop(1, ranks, project, 0)

    def attend_old(b):
        found = stack(
            [
                lax.dot_general(
                    spread[n, b],
                    old_keys[b, :, n * two_heads : (n + 1) * two_heads],
                    nt,
                    preferred_element_type=F32,
                )
                for n in range(heads // FOLD)
            ]
        )
        place = rank * context_dev + iota((1, context_dev), 1)
        found = jnp.where(place < lengths[b], found, masked_score)
        peak = jnp.max(found, axis=-1, keepdims=True)
        exact = jnp.exp2((found - peak) * log_scale)
        amount = jnp.sum(exact, axis=-1, keepdims=True)
        exact = exact.astype(BF16)
        for n in range(heads // FOLD):
            summed = jnp.dot(
                exact[n * FOLD : (n + 1) * FOLD],
                old_values[b, :, n * two_heads : (n + 1) * two_heads],
                preferred_element_type=F32,
            )
            for i in range(FOLD // local_heads):
                h = i * local_heads // per_kv
                old_wide[
                    n * (FOLD // local_heads) + i, b * local_heads : (b + 1) * local_heads
                ] = summed[
                    i * local_heads : (i + 1) * local_heads,
                    h * HEAD_WIDTH : (h + 1) * HEAD_WIDTH,
                ]
        return jnp.where(lane == b, peak * log_scale, jnp.where(lane == rows + b, amount, 0.0))

    def softmax(p):
        sums = []
        for c in range(BOUNDS[p], BOUNDS[p + 1]):
            total = own_sums[c]
            arrived(incoming.at[c, other_chips], got_sum.at[c])
            for step in range(1, chips):
                other = chip_at(step)[0]
                total = total + unfold(incoming[c, other].astype(F32), local_heads)
            sums.append(total)
        total = beside(sums)
        slot = beside(
            [
                slot_of[t][:local_heads]
                for t in range(BOUNDS[p] * per_chunk, BOUNDS[p + 1] * per_chunk)
            ]
        )
        peak_of, peaks = jnp.zeros_like(total), []
        for o in range(groups):
            owned = (slot >= o * per_owner) & (slot < (o + 1) * per_owner)
            peak = jnp.max(jnp.where(owned, total, masked_score), axis=-1, keepdims=True)
            peak_of = jnp.where(owned, peak, peak_of)
            peaks.append(peak * log_scale)
        exact = jnp.exp2((total - peak_of) * log_scale)
        weights[p][rank] = fold(exact).astype(BF16)
        for step in range(1, chips):
            weight_copy(step, p).start()
        on_copy(0, p).start()
        for o in range(groups):
            owned = (slot >= o * per_owner) & (slot < (o + 1) * per_owner)
            amount = jnp.sum(jnp.where(owned, exact, 0.0), axis=-1, keepdims=True)
            cross_out[o, p] = jnp.where(lane < half, peaks[o], amount)

    def pass_on(p):
        arrived(weights[p].at[other_chips], got_weight.at[p])
        for step in range(1, chips):
            on_copy(step, p).start()

    def mix(p):
        arrived(weights[p].at[pl.ds(0, chips)], got_on.at[p])
        width = weights[p].shape[2]
        base = BOUNDS[p] * chunk
        part = (BOUNDS[p + 1] - BOUNDS[p]) * chunk
        for q in range(FOLD // local_heads):
            every = stack(
                [
                    weights[p][j].astype(F32)[q * local_heads : (q + 1) * local_heads]
                    for j in range(ranks)
                ]
            )
            for u in range(width // block):
                start = q * width + u * block
                slot = slot_of[(base + start) // block][0:1]
                values = every[:, u * block : (u + 1) * block]
                for o in range(groups):
                    owned = (slot >= o * per_owner) & (slot < (o + 1) * per_owner)
                    masked[o * heads : (o + 1) * heads, start : start + block] = jnp.where(
                        owned, values, 0.0
                    ).astype(BF16)
        wide = 2 * HEAD_WIDTH
        for n in range(features // wide):
            mixed[:, n * wide : (n + 1) * wide] = jnp.dot(
                masked[:, :part],
                x[base : base + part, n * wide : (n + 1) * wide],
                preferred_element_type=F32,
            ).astype(BF16)
        tall = 2 * per_kv
        for n in range(kv_heads // 2):
            left = stack(
                [
                    mixed[o * heads + n * tall : o * heads + (n + 1) * tall, :]
                    for o in range(groups)
                ]
            )
            found = jnp.dot(left, wv[:, n * wide : (n + 1) * wide], preferred_element_type=F32)
            for i in range(tall // local_heads):
                h = i * local_heads // per_kv
                first = p * (FOLD // PARTS)
                for o in range(groups):
                    at = o * tall + i * local_heads
                    fresh_wide[o * ranks + n * (tall // local_heads) + i, first : first + local_heads] = found[
                        at : at + local_heads, h * HEAD_WIDTH : (h + 1) * HEAD_WIDTH
                    ]

    old_key_load.wait()
    old_value_load.wait()
    about = attend_old(0)
    add_pair(CHUNKS - 1)
    for b in range(1, rows // 2):
        about = about + attend_old(b)
    softmax(0)
    for b in range(rows // 2, rows):
        about = about + attend_old(b)
    softmax(1)
    for step in range(1, groups):
        cross_copy(step).start()
    cross_in[group] = cross_out[group]
    for j in range(ranks):
        old_out[j] = old_wide[j].astype(BF16)
        old_stat_out[j] = about[j * local_heads : (j + 1) * local_heads]
    pass_on(0)
    pass_on(1)
    for step in range(1, ranks):
        for copy in old_copies(step):
            copy.start()
    value_load.wait()
    mix(0)
    mix(1)
    fresh_out[...] = fresh_wide[...].astype(BF16)

    def start(step, carry):
        fresh_copy(step).start()
        return carry

    lax.fori_loop(1, groups * ranks, start, 0)
    fresh_in[own] = fresh_out[own]

    old_in[rank] = old_out[rank]
    old_stat_in[rank] = old_stat_out[rank]
    arrived(old_in.at[other_ranks], got_old)
    arrived(old_stat_in.at[other_ranks], got_stat)
    held = []
    for b in range(rows):
        tops = [old_stat_in[r][:, b : b + 1] for r in range(ranks)]
        top = functools.reduce(jnp.maximum, tops)
        numerator, denominator = 0.0, 0.0
        for r in range(ranks):
            factor = jnp.exp2(tops[r] - top)
            numerator = numerator + factor * old_in[r].astype(F32)[
                b * local_heads : (b + 1) * local_heads
            ]
            denominator = denominator + factor * old_stat_in[r][:, rows + b : rows + b + 1]
        held.append((top, numerator, denominator))

    arrived(cross_in.at[other_groups], got_cross)
    found = [[item] for item in held]
    arrived(fresh_in.at[pl.ds(1, groups * ranks - 1)], got_fresh)
    for source in range(groups):
        total = jnp.sum(fresh_in[source * ranks : (source + 1) * ranks].astype(F32), axis=0)
        for p in range(PARTS):
            stat = cross_in[source, p]
            first = p * (FOLD // PARTS)
            found[source // senders].append(
                (stat[:, 0:1], total[first : first + local_heads], stat[:, half : half + 1])
            )
    for b in range(rows):
        top = functools.reduce(jnp.maximum, [item[0] for item in found[b]])
        numerator, denominator = 0.0, 0.0
        for peak, value, amount in found[b]:
            factor = jnp.exp2(peak - top)
            numerator = numerator + factor * value
            denominator = denominator + factor * amount
        out[b] = (numerator / denominator).astype(out.dtype)

    left(slots.at[other_ranks], send_slot)
    left(query_all.at[other_ranks], send_query)
    left(far_all.at[other_ranks], send_near)
    left(far_in.at[other_groups], send_far)
    left(old_in.at[other_ranks], send_old)
    left(old_stat_in.at[other_ranks], send_stat)
    left(cross_in.at[other_groups], send_cross)
    left(fresh_in.at[pl.ds(1, groups * ranks - 1)], send_fresh)
    left(paired, send_pair)
    left(incoming.at[:, other_chips], send_sum)
    for p in range(PARTS):
        left(weights[p].at[other_chips], send_weight.at[p])
        left(weights[p].at[pl.ds(0, chips)], send_on.at[p])


def per_device(
    prefill_states, key_weight, value_weight, page_slot, decode_states, query_weight,
    cache_keys, cache_values, cached_length,
):
    groups = lax.axis_size("group")
    ranks = lax.axis_size("tensor")
    chips = ranks // 2
    tokens, features = prefill_states.shape
    kv_width = key_weight.shape[1]
    block = tokens // ranks
    pages = block // PAGE
    rows, model = decode_states.shape
    width = query_weight.shape[1]
    local_heads = width // HEAD_WIDTH
    heads = local_heads * ranks
    chunk = tokens // CHUNKS
    widths = [
        local_heads * chunk * (BOUNDS[p + 1] - BOUNDS[p]) // FOLD for p in range(PARTS)
    ]
    longest = chunk * max(BOUNDS[p + 1] - BOUNDS[p] for p in range(PARTS))
    dma = pltpu.SemaphoreType.DMA
    vmem = pltpu.VMEM
    hbm = pl.BlockSpec(memory_space=pltpu.HBM)
    result = pl.pallas_call(
        functools.partial(body, groups, ranks),
        in_specs=[hbm] * 9,
        out_specs=pl.BlockSpec(memory_space=pltpu.VMEM),
        out_shape=jax.ShapeDtypeStruct((rows, local_heads, HEAD_WIDTH), BF16),
        scratch_shapes=[
            vmem((tokens, features), BF16),
            vmem((features, kv_width), BF16),
            vmem((features, kv_width), BF16),
            vmem(query_weight.shape, BF16),
            vmem(cache_keys.shape, BF16),
            vmem(cache_values.shape, BF16),
            vmem(page_slot.shape, jnp.int32),
            vmem(decode_states.shape, BF16),
            pltpu.SMEM((rows,), jnp.int32),
            vmem((ranks, PAGE, pages), F32),
            vmem((ranks, PAGE, block), F32),
            vmem((ranks, PAGE, HEAD_WIDTH), F32),
            vmem((ranks, PAGE, HEAD_WIDTH), F32),
            vmem((pages, 4 * HEAD_WIDTH), BF16),
            vmem((groups, local_heads, HEAD_WIDTH), F32),
            vmem((groups, local_heads, HEAD_WIDTH), F32),
            vmem((ranks, rows * local_heads, HEAD_WIDTH), BF16),
            vmem((ranks, groups * local_heads, HEAD_WIDTH), BF16),
            vmem((heads // FOLD, rows + groups, FOLD, 2 * HEAD_WIDTH), BF16),
            vmem((tokens, kv_width), BF16),
            vmem((2, CHUNKS, chips, local_heads, chunk), F32),
            vmem((CHUNKS, chips, local_heads, chunk), F32),
            vmem((CHUNKS, chips, FOLD, local_heads * chunk // FOLD), BF16),
            vmem((CHUNKS, chips, FOLD, local_heads * chunk // FOLD), BF16),
            vmem((CHUNKS, local_heads, chunk), F32),
            vmem((ranks, FOLD, widths[0]), BF16),
            vmem((ranks, FOLD, widths[1]), BF16),
            vmem((groups * heads, longest), BF16),
            vmem((groups * heads, features), BF16),
            vmem((groups * ranks, FOLD, HEAD_WIDTH), F32),
            vmem((groups * ranks, FOLD, HEAD_WIDTH), BF16),
            vmem((groups * ranks, FOLD, HEAD_WIDTH), BF16),
            vmem((ranks, rows * local_heads, HEAD_WIDTH), F32),
            vmem((ranks, rows * local_heads, HEAD_WIDTH), BF16),
            vmem((ranks, rows * local_heads, HEAD_WIDTH), BF16),
            vmem((ranks, local_heads, HEAD_WIDTH), F32),
            vmem((ranks, local_heads, HEAD_WIDTH), F32),
            vmem((groups, PARTS, local_heads, HEAD_WIDTH), F32),
            vmem((groups, PARTS, local_heads, HEAD_WIDTH), F32),
            dma((ranks,)), dma((7,)), dma((PIECES,)),
            dma, dma, dma, dma, dma, dma, dma, dma,
            dma, dma((CHUNKS,)), dma, dma((CHUNKS,)),
            dma((PARTS,)), dma((PARTS,)), dma((PARTS,)), dma((PARTS,)),
            dma, dma, dma, dma, dma, dma, dma, dma,
        ],
        compiler_params=pltpu.CompilerParams(
            collective_id=0, has_side_effects=True, vmem_limit_bytes=58 * 1024 * 1024
        ),
    )(
        prefill_states, key_weight, value_weight, page_slot, decode_states, query_weight,
        cache_keys, cache_values, cached_length,
    )
    return result.reshape(rows, local_heads * HEAD_WIDTH)


def solution(mesh):
    placed = (
        P("group", "tensor"),
        P("tensor", None),
        P("tensor", None),
        P("group", "tensor", None),
        P("group", None),
        P(None, "tensor"),
        P("group", "tensor", None),
        P("group", "tensor", None),
        P("group"),
    )
    return jax.shard_map(
        per_device, mesh=mesh, in_specs=placed, out_specs=P("group", "tensor"), check_vma=False
    )
```

```python
import functools
import math

import jax
import jax.numpy as jnp
from jax import lax
from jax.experimental import pallas as pl
from jax.experimental.pallas import tpu as pltpu
from jax.sharding import PartitionSpec as P

HEAD_WIDTH = 128
PAGE = 8
FOLD = 16
CHUNKS = 4
PARTS = 2
BOUNDS = (0, 2, 4)
PIECES = 4

rope_theta = 500000.0
masked_score = -1e30
F32, BF16 = jnp.float32, jnp.bfloat16


def log2_of(number):
    power = number.bit_length() - 1
    assert 1 << power == number
    return power


def remote(src, dst, send_sem, recv_sem, group, rank):
    return pltpu.make_async_remote_copy(
        src_ref=src,
        dst_ref=dst,
        send_sem=send_sem,
        recv_sem=recv_sem,
        device_id={"group": group, "tensor": rank},
        device_id_type=pl.DeviceIdType.MESH,
    )


def stack(pieces):
    return pieces[0] if len(pieces) == 1 else jnp.concatenate(pieces, axis=0)


def beside(pieces):
    return pieces[0] if len(pieces) == 1 else jnp.concatenate(pieces, axis=1)


def fold(values):
    count = FOLD // values.shape[0]
    width = values.shape[1] // count
    return stack([values[:, q * width : (q + 1) * width] for q in range(count)])


def unfold(values, height):
    return beside([values[q : q + height] for q in range(0, FOLD, height)])


def iota(shape, axis):
    return lax.broadcasted_iota(jnp.int32, shape, axis)


def body(
    groups, ranks,
    states, key_weight, value_weight, page_slot, decode, query_weight, cache_keys, cache_values,
    cached_length,
    out,
    x, wk, wv, wq, old_keys, old_values, slot_in, decode_in, lengths,
    slots, slot_of, step_cos, step_sin, page_table, far_out, far_in,
    query_all, far_all, spread, keys,
    partial, paired, chip_sums, incoming, own_sums,
    weights_0, weights_1, masked, mixed, fresh_wide, fresh_out, fresh_in,
    old_wide, old_out, old_in, old_stat_out, old_stat_in, cross_out, cross_in,
    x_sems, load_sems, wq_sems,
    send_slot, got_slot, send_far, got_far, send_query, got_query, send_near, got_near,
    send_pair, got_pair, send_sum, got_sum, send_weight, got_weight, send_on, got_on,
    send_fresh, got_fresh, send_old, got_old, send_stat, got_stat, send_cross, got_cross,
):
    group, rank = lax.axis_index("group"), lax.axis_index("tensor")
    chips = ranks // 2
    core, chip = lax.rem(rank, 2), rank // 2
    partner = chip * 2 + 1 - core
    own = group * ranks + rank
    tokens, features = x.shape
    block = tokens // ranks
    pages = block // PAGE
    per_owner = pages // groups
    rows, context_dev, kv_width = old_keys.shape
    kv_heads = kv_width // HEAD_WIDTH
    local_heads = out.shape[1]
    heads = local_heads * ranks
    per_kv = heads // kv_heads
    share, span = block // groups, block // rows
    senders = span // share
    offset = lax.rem(group, senders) * share
    query_rows = 2 * rows
    depth = wq.shape[0] // PIECES
    weights = (weights_0, weights_1)
    chunk = tokens // CHUNKS
    per_chunk = chunk // block
    two_heads = 2 * HEAD_WIDTH
    assert FOLD == 2 * per_kv
    log_scale = math.log2(math.e) / HEAD_WIDTH**0.5
    half = HEAD_WIDTH // 2

    def rank_at(step):
        return lax.rem(rank + step, ranks)

    def group_at(step):
        return lax.rem(group + step, groups)

    def chip_at(step):
        other = lax.rem(chip + step, chips)
        return other, other * 2 + core

    def x_copy(step):
        start = pl.ds(pl.multiple_of(step * block, block), block)
        return pltpu.make_async_copy(states.at[start, :], x.at[start, :], x_sems.at[step])

    def query_load(i):
        span_i = pl.ds(i * depth, depth)
        return pltpu.make_async_copy(query_weight.at[span_i, :], wq.at[span_i, :], wq_sems.at[i])

    def load(source, target, index):
        return pltpu.make_async_copy(source, target, load_sems.at[index])

    key_load = load(key_weight, wk, 0)
    slot_load = load(page_slot, slot_in, 1)
    decode_load = load(decode, decode_in, 2)
    length_load = load(cached_length, lengths, 3)
    value_load = load(value_weight, wv, 4)
    old_key_load = load(cache_keys, old_keys, 5)
    old_value_load = load(cache_values, old_values, 6)

    slot_load.start()
    decode_load.start()
    length_load.start()
    key_load.start()
    x_copy(rank).start()
    query_load(0).start()

    barrier = pltpu.get_barrier_semaphore()

    def greet(peer_group, peer_rank):
        pl.semaphore_signal(
            barrier,
            inc=1,
            device_id={"group": peer_group, "tensor": peer_rank},
            device_id_type=pl.DeviceIdType.MESH,
        )

    for step in range(1, groups):
        greet(group_at(step), rank)
    for step in range(1, ranks):
        greet(group, rank_at(step))

    def slot_copy(step):
        return remote(
            slots.at[rank], slots.at[rank], send_slot, got_slot,
            group, rank_at(step),
        )

    def far_copy(step):
        peer = group_at(step)
        return remote(
            far_out.at[peer], far_in.at[group], send_far, got_far, peer, rank
        )

    def near_copy(step):
        return remote(
            far_all.at[rank], far_all.at[rank], send_near, got_near,
            group, rank_at(step),
        )

    def query_copy(step):
        return remote(
            query_all.at[rank], query_all.at[rank], send_query, got_query,
            group, rank_at(step),
        )

    def pair_copy(c):
        return remote(
            partial.at[1 - core, c], paired.at[c], send_pair, got_pair.at[c], group, partner
        )

    def sum_copy(step, c):
        other, peer = chip_at(step)
        return remote(
            chip_sums.at[c, other], incoming.at[c, chip], send_sum, got_sum.at[c], group, peer,
        )

    def weight_copy(step, p):
        other, peer = chip_at(step)
        return remote(
            weights[p].at[rank], weights[p].at[rank], send_weight.at[p],
            got_weight.at[p], group, peer,
        )

    def on_copy(step, p):
        other, peer = chip_at(step)
        return remote(
            weights[p].at[peer], weights[p].at[peer], send_on.at[p],
            got_on.at[p], group, partner,
        )

    def other_at(step):
        peer = lax.rem(own + step, groups * ranks)
        return peer // ranks, lax.rem(peer, ranks)

    def fresh_copy(step):
        peer_group, peer_rank = other_at(step)
        return remote(
            fresh_out.at[peer_group * ranks + peer_rank], fresh_in.at[own],
            send_fresh, got_fresh, peer_group, peer_rank,
        )

    def old_copies(step):
        peer = rank_at(step)
        return (
            remote(
                old_out.at[peer], old_in.at[rank], send_old, got_old, group, peer
            ),
            remote(
                old_stat_out.at[peer], old_stat_in.at[rank], send_stat, got_stat, group, peer,
            ),
        )

    def cross_copy(step):
        peer = group_at(step)
        return remote(
            cross_out.at[peer], cross_in.at[group], send_cross, got_cross,
            peer, rank,
        )

    def arrived(ref, semaphore):
        remote(ref, ref, semaphore, semaphore, group, partner).wait_recv()

    def left(ref, semaphore):
        remote(ref, ref, semaphore, semaphore, group, partner).wait_send()

    other_ranks, other_groups = pl.ds(1, ranks - 1), pl.ds(1, groups - 1)
    other_chips = pl.ds(1, chips - 1)

    lane = iota((1, HEAD_WIDTH), 1)
    sign = jnp.where(lane < half, -1.0, 1.0).astype(F32)
    frequency = jnp.exp(
        jnp.where(lane < half, lane, lane - half).astype(F32)
        * (-2.0 * math.log(rope_theta) / HEAD_WIDTH)
    )
    line = iota((ranks * PAGE, HEAD_WIDTH), 0)
    start = (line >> log2_of(PAGE)) * span + (line & (PAGE - 1)) + offset
    step_angle = start.astype(F32) * frequency
    step_cos[...] = jnp.cos(step_angle).reshape(step_cos.shape)
    step_sin[...] = jnp.sin(step_angle).reshape(step_sin.shape)
    line = iota((pages, HEAD_WIDTH), 0)
    page_angle = ((line & (per_owner - 1)) * PAGE).astype(F32) * frequency
    for i, table in enumerate((jnp.cos(page_angle), jnp.sin(page_angle))):
        high = table.astype(BF16)
        page_table[:, 2 * i * HEAD_WIDTH : (2 * i + 1) * HEAD_WIDTH] = high
        page_table[:, (2 * i + 1) * HEAD_WIDTH : (2 * i + 2) * HEAD_WIDTH] = (
            table - high.astype(F32)
        ).astype(BF16)
    slot_load.wait()
    slots[rank] = jnp.broadcast_to(slot_in[0].astype(F32), (PAGE, pages))
    length_load.wait()
    query_row = iota((query_rows, HEAD_WIDTH), 0)
    position = jnp.zeros((query_rows, HEAD_WIDTH), jnp.int32)
    for b in range(rows):
        position = jnp.where(query_row == b, lengths[b], position)
    query_angle = (position + ranks * span).astype(F32) * frequency
    query_cos, query_sin = jnp.cos(query_angle), jnp.sin(query_angle) * sign
    on_diagonal = iota((pages, pages), 0) == iota((pages, pages), 1)
    page_lane = iota((pages, pages), 1).astype(F32)

    def project_keys(t):
        tokens_t = pl.ds(pl.multiple_of(t * block, block), block)
        row = jnp.broadcast_to(slots[t][0:1], (pages, pages))
        column = jnp.sum(jnp.where(on_diagonal, row, 0.0), axis=1, keepdims=True)
        chosen = jnp.where(page_lane == column, 1.0, 0.0).astype(BF16)
        table = jnp.dot(chosen, page_table[...], preferred_element_type=F32)
        big_cos = (table[:, :HEAD_WIDTH] + table[:, HEAD_WIDTH : 2 * HEAD_WIDTH]).reshape(
            pages, 1, HEAD_WIDTH
        )
        big_sin = (
            table[:, 2 * HEAD_WIDTH : 3 * HEAD_WIDTH] + table[:, 3 * HEAD_WIDTH :]
        ).reshape(pages, 1, HEAD_WIDTH)
        small_cos = step_cos[t].reshape(1, PAGE, HEAD_WIDTH)
        small_sin = step_sin[t].reshape(1, PAGE, HEAD_WIDTH)
        cosine = (big_cos * small_cos - big_sin * small_sin).reshape(block, HEAD_WIDTH)
        sine = (big_sin * small_cos + big_cos * small_sin).reshape(block, HEAD_WIDTH) * sign
        wide = 2 * HEAD_WIDTH
        for n in range(kv_width // wide):
            found = jnp.dot(
                x[tokens_t, :], wk[:, n * wide : (n + 1) * wide], preferred_element_type=F32
            )
            for i in range(2):
                head = found[:, i * HEAD_WIDTH : (i + 1) * HEAD_WIDTH]
                start = n * wide + i * HEAD_WIDTH
                keys[tokens_t, start : start + HEAD_WIDTH] = (
                    head * cosine + pltpu.roll(head, half, 1) * sine
                ).astype(BF16)

    def turn_near():
        arrived(far_in.at[other_groups], got_far)
        far_all[rank] = stack([far_in[o] for o in range(groups)]).astype(BF16)
        for step in range(1, ranks):
            near_copy(step).start()

    def spread_queries():
        arrived(far_all.at[other_ranks], got_near)
        arrived(query_all.at[other_ranks], got_query)
        per_tile = FOLD // local_heads
        for r in range(rows + groups):
            held, at = (query_all, r) if r < rows else (far_all, r - rows)
            for u in range(heads // FOLD):
                members = range(u * per_tile, (u + 1) * per_tile)
                taken = [
                    held[j].astype(F32)[at * local_heads : (at + 1) * local_heads]
                    for j in members
                ]
                for h in sorted({j * local_heads // per_kv for j in members}):
                    first = h * HEAD_WIDTH - u * two_heads
                    spread[u, r, :, first : first + HEAD_WIDTH] = stack(
                        [
                            value if j * local_heads // per_kv == h else jnp.zeros_like(value)
                            for j, value in zip(members, taken)
                        ]
                    ).astype(BF16)

    def add_pair(c):
        arrived(paired.at[c], got_pair.at[c])
        for k in range(chips):
            chip_sums[c, k] = fold(partial[core, c, k] + paired[c, k]).astype(BF16)
        for step in range(1, chips):
            sum_copy(step, c).start()
        own_sums[c] = partial[core, c, chip] + paired[c, chip]

    nt = (((1,), (1,)), ((), ()))

    def score(first, c, carry):
        for u in range(per_chunk):
            t = c * per_chunk + u
            slot = slot_of[t][0:1]
            for n in range(heads // FOLD):
                found = lax.dot_general(
                    spread[n, rows:].reshape(groups * FOLD, two_heads),
                    keys[
                        pl.ds(pl.multiple_of(t * block, block), block),
                        n * two_heads : (n + 1) * two_heads,
                    ],
                    nt,
                    preferred_element_type=F32,
                )
                kept = found[:FOLD]
                for o in range(1, groups):
                    kept = jnp.where(
                        slot >= o * per_owner, found[o * FOLD : (o + 1) * FOLD], kept
                    )
                for i in range(FOLD // local_heads):
                    j = n * (FOLD // local_heads) + i
                    partial[j % 2, c, j // 2, :, u * block : (u + 1) * block] = kept[
                        i * local_heads : (i + 1) * local_heads
                    ]
        pair_copy(c).start()

        @pl.when(c > first)
        def _():
            add_pair(c - 1)

        return carry

    def block_at(tick):
        return jnp.where(tick - 1 < rank, tick - 1, tick)

    key_load.wait()
    x_copy(rank).wait()
    for i in range(1, PIECES):
        query_load(i).start()
    project_keys(rank)
    pl.semaphore_wait(barrier, groups + ranks - 2)
    for step in range(1, ranks):
        slot_copy(step).start()
    decode_load.wait()
    turns = depth // min(depth, 1024)

    def add_piece(i, total):
        span_i = pl.ds(pl.multiple_of(i * (depth // turns), depth // turns), depth // turns)
        return total + jnp.dot(
            decode_in[:, span_i], wq[span_i, :], preferred_element_type=F32
        )

    total = jnp.zeros((rows, wq.shape[1]), F32)
    for i in range(PIECES):
        query_load(i).wait()
        total = lax.fori_loop(i * turns, (i + 1) * turns, add_piece, total)
        if i == PIECES - 2:
            for tick in range(1, ranks):
                x_copy(block_at(tick)).start()
    total = stack([total, total])
    turned = []
    for h in range(local_heads):
        head = total[:, h * HEAD_WIDTH : (h + 1) * HEAD_WIDTH]
        turned.append(head * query_cos + pltpu.roll(head, half, 1) * query_sin)
    size = local_heads * query_rows
    m, k = iota((size, size), 0), iota((size, size), 1)
    order = (m >> log2_of(local_heads) == k & (query_rows - 1)) & (
        m & (local_heads - 1) == k >> log2_of(query_rows)
    )
    arranged = jnp.dot(
        jnp.where(order, 1.0, 0.0).astype(BF16),
        stack(turned).astype(BF16),
        preferred_element_type=F32,
    )
    for g in range(groups):
        at = (rows + g // senders) * local_heads
        far_out[g] = arranged[at : at + local_heads]
    for step in range(1, groups):
        far_copy(step).start()
    query_all[rank] = arranged[: rows * local_heads].astype(BF16)
    for step in range(1, ranks):
        query_copy(step).start()
    far_in[group] = far_out[group]
    value_load.start()
    old_key_load.start()
    old_value_load.start()
    arrived(slots.at[other_ranks], got_slot)
    widen = (
        (iota((pages, block), 1) >> log2_of(PAGE)) == iota((pages, block), 0)
    ).astype(BF16)
    slot_of[...] = jnp.dot(
        slots[...].reshape(ranks * PAGE, pages).astype(BF16), widen, preferred_element_type=F32
    ).reshape(ranks, PAGE, block)

    near_tick, score_tick = 3 * ranks // 8, ranks - 3

    def scored(tick):
        ready = jnp.where(tick == ranks - 1, CHUNKS, tick // per_chunk)
        return jnp.where(tick < score_tick, 0, ready)

    def project(tick, carry):
        @pl.when(tick == near_tick)
        def _():
            turn_near()

        t = block_at(tick)
        x_copy(t).wait()
        project_keys(t)
        before, first, last = scored(tick - 2), scored(tick - 1), scored(tick)

        @pl.when(first > before)
        def _():
            add_pair(first - 1)

        @pl.when(tick == score_tick)
        def _():
            spread_queries()

        lax.fori_loop(first, last, functools.partial(score, first), 0)
        return carry

    lax.fori_loop(1, ranks, project, 0)

    def attend_old(b):
        found = stack(
            [
                lax.dot_general(
                    spread[n, b],
                    old_keys[b, :, n * two_heads : (n + 1) * two_heads],
                    nt,
                    preferred_element_type=F32,
                )
                for n in range(heads // FOLD)
            ]
        )
        place = rank * context_dev + iota((1, context_dev), 1)
        found = jnp.where(place < lengths[b], found, masked_score)
        peak = jnp.max(found, axis=-1, keepdims=True)
        exact = jnp.exp2((found - peak) * log_scale)
        amount = jnp.sum(exact, axis=-1, keepdims=True)
        exact = exact.astype(BF16)
        for n in range(heads // FOLD):
            summed = jnp.dot(
                exact[n * FOLD : (n + 1) * FOLD],
                old_values[b, :, n * two_heads : (n + 1) * two_heads],
                preferred_element_type=F32,
            )
            for i in range(FOLD // local_heads):
                h = i * local_heads // per_kv
                old_wide[
                    n * (FOLD // local_heads) + i, b * local_heads : (b + 1) * local_heads
                ] = summed[
                    i * local_heads : (i + 1) * local_heads,
                    h * HEAD_WIDTH : (h + 1) * HEAD_WIDTH,
                ]
        return jnp.where(lane == b, peak * log_scale, jnp.where(lane == rows + b, amount, 0.0))

    def softmax(p):
        sums = []
        for c in range(BOUNDS[p], BOUNDS[p + 1]):
            total = own_sums[c]
            arrived(incoming.at[c, other_chips], got_sum.at[c])
            for step in range(1, chips):
                other = chip_at(step)[0]
                total = total + unfold(incoming[c, other].astype(F32), local_heads)
            sums.append(total)
        total = beside(sums)
        slot = beside(
            [
                slot_of[t][:local_heads]
                for t in range(BOUNDS[p] * per_chunk, BOUNDS[p + 1] * per_chunk)
            ]
        )
        peak_of, peaks = jnp.zeros_like(total), []
        for o in range(groups):
            owned = (slot >= o * per_owner) & (slot < (o + 1) * per_owner)
            peak = jnp.max(jnp.where(owned, total, masked_score), axis=-1, keepdims=True)
            peak_of = jnp.where(owned, peak, peak_of)
            peaks.append(peak * log_scale)
        exact = jnp.exp2((total - peak_of) * log_scale)
        weights[p][rank] = fold(exact).astype(BF16)
        for step in range(1, chips):
            weight_copy(step, p).start()
        on_copy(0, p).start()
        for o in range(groups):
            owned = (slot >= o * per_owner) & (slot < (o + 1) * per_owner)
            amount = jnp.sum(jnp.where(owned, exact, 0.0), axis=-1, keepdims=True)
            cross_out[o, p] = jnp.where(lane < half, peaks[o], amount)

    def pass_on(p):
        arrived(weights[p].at[other_chips], got_weight.at[p])
        for step in range(1, chips):
            on_copy(step, p).start()

    def mix(p):
        arrived(weights[p].at[pl.ds(0, chips)], got_on.at[p])
        width = weights[p].shape[2]
        base = BOUNDS[p] * chunk
        part = (BOUNDS[p + 1] - BOUNDS[p]) * chunk
        for q in range(FOLD // local_heads):
            every = stack(
                [
                    weights[p][j].astype(F32)[q * local_heads : (q + 1) * local_heads]
                    for j in range(ranks)
                ]
            )
            for u in range(width // block):
                start = q * width + u * block
                slot = slot_of[(base + start) // block][0:1]
                values = every[:, u * block : (u + 1) * block]
                for o in range(groups):
                    owned = (slot >= o * per_owner) & (slot < (o + 1) * per_owner)
                    masked[o * heads : (o + 1) * heads, start : start + block] = jnp.where(
                        owned, values, 0.0
                    ).astype(BF16)
        wide = 2 * HEAD_WIDTH
        for n in range(features // wide):
            mixed[:, n * wide : (n + 1) * wide] = jnp.dot(
                masked[:, :part],
                x[base : base + part, n * wide : (n + 1) * wide],
                preferred_element_type=F32,
            ).astype(BF16)
        tall = 2 * per_kv
        for n in range(kv_heads // 2):
            left = stack(
                [
                    mixed[o * heads + n * tall : o * heads + (n + 1) * tall, :]
                    for o in range(groups)
                ]
            )
            found = jnp.dot(left, wv[:, n * wide : (n + 1) * wide], preferred_element_type=F32)
            for i in range(tall // local_heads):
                h = i * local_heads // per_kv
                first = p * (FOLD // PARTS)
                for o in range(groups):
                    at = o * tall + i * local_heads
                    fresh_wide[o * ranks + n * (tall // local_heads) + i, first : first + local_heads] = found[
                        at : at + local_heads, h * HEAD_WIDTH : (h + 1) * HEAD_WIDTH
                    ]

    old_key_load.wait()
    old_value_load.wait()
    about = attend_old(0)
    add_pair(CHUNKS - 1)
    for b in range(1, rows // 2):
        about = about + attend_old(b)
    softmax(0)
    for b in range(rows // 2, rows):
        about = about + attend_old(b)
    softmax(1)
    for step in range(1, groups):
        cross_copy(step).start()
    cross_in[group] = cross_out[group]
    for j in range(ranks):
        old_out[j] = old_wide[j].astype(BF16)
        old_stat_out[j] = about[j * local_heads : (j + 1) * local_heads]
    pass_on(0)
    pass_on(1)
    for step in range(1, ranks):
        for copy in old_copies(step):
            copy.start()
    value_load.wait()
    mix(0)
    mix(1)
    fresh_out[...] = fresh_wide[...].astype(BF16)

    def start(step, carry):
        fresh_copy(step).start()
        return carry

    lax.fori_loop(1, groups * ranks, start, 0)
    fresh_in[own] = fresh_out[own]

    old_in[rank] = old_out[rank]
    old_stat_in[rank] = old_stat_out[rank]
    arrived(old_in.at[other_ranks], got_old)
    arrived(old_stat_in.at[other_ranks], got_stat)
    held = []
    for b in range(rows):
        tops = [old_stat_in[r][:, b : b + 1] for r in range(ranks)]
        top = functools.reduce(jnp.maximum, tops)
        numerator, denominator = 0.0, 0.0
        for r in range(ranks):
            factor = jnp.exp2(tops[r] - top)
            numerator = numerator + factor * old_in[r].astype(F32)[
                b * local_heads : (b + 1) * local_heads
            ]
            denominator = denominator + factor * old_stat_in[r][:, rows + b : rows + b + 1]
        held.append((top, numerator, denominator))

    arrived(cross_in.at[other_groups], got_cross)
    found = [[item] for item in held]
    arrived(fresh_in.at[pl.ds(1, groups * ranks - 1)], got_fresh)
    for source in range(groups):
        total = jnp.sum(fresh_in[source * ranks : (source + 1) * ranks].astype(F32), axis=0)
        for p in range(PARTS):
            stat = cross_in[source, p]
            first = p * (FOLD // PARTS)
            found[source // senders].append(
                (stat[:, 0:1], total[first : first + local_heads], stat[:, half : half + 1])
            )
    for b in range(rows):
        top = functools.reduce(jnp.maximum, [item[0] for item in found[b]])
        numerator, denominator = 0.0, 0.0
        for peak, value, amount in found[b]:
            factor = jnp.exp2(peak - top)
            numerator = numerator + factor * value
            denominator = denominator + factor * amount
        out[b] = (numerator / denominator).astype(out.dtype)

    left(slots.at[other_ranks], send_slot)
    left(query_all.at[other_ranks], send_query)
    left(far_all.at[other_ranks], send_near)
    left(far_in.at[other_groups], send_far)
    left(old_in.at[other_ranks], send_old)
    left(old_stat_in.at[other_ranks], send_stat)
    left(cross_in.at[other_groups], send_cross)
    left(fresh_in.at[pl.ds(1, groups * ranks - 1)], send_fresh)
    left(paired, send_pair)
    left(incoming.at[:, other_chips], send_sum)
    for p in range(PARTS):
        left(weights[p].at[other_chips], send_weight.at[p])
        left(weights[p].at[pl.ds(0, chips)], send_on.at[p])


def per_device(
    prefill_states, key_weight, value_weight, page_slot, decode_states, query_weight,
    cache_keys, cache_values, cached_length,
):
    groups = lax.axis_size("group")
    ranks = lax.axis_size("tensor")
    chips = ranks // 2
    tokens, features = prefill_states.shape
    kv_width = key_weight.shape[1]
    block = tokens // ranks
    pages = block // PAGE
    rows, model = decode_states.shape
    width = query_weight.shape[1]
    local_heads = width // HEAD_WIDTH
    heads = local_heads * ranks
    chunk = tokens // CHUNKS
    widths = [
        local_heads * chunk * (BOUNDS[p + 1] - BOUNDS[p]) // FOLD for p in range(PARTS)
    ]
    longest = chunk * max(BOUNDS[p + 1] - BOUNDS[p] for p in range(PARTS))
    dma = pltpu.SemaphoreType.DMA
    vmem = pltpu.VMEM
    hbm = pl.BlockSpec(memory_space=pltpu.HBM)
    result = pl.pallas_call(
        functools.partial(body, groups, ranks),
        in_specs=[hbm] * 9,
        out_specs=pl.BlockSpec(memory_space=pltpu.VMEM),
        out_shape=jax.ShapeDtypeStruct((rows, local_heads, HEAD_WIDTH), BF16),
        scratch_shapes=[
            vmem((tokens, features), BF16),
            vmem((features, kv_width), BF16),
            vmem((features, kv_width), BF16),
            vmem(query_weight.shape, BF16),
            vmem(cache_keys.shape, BF16),
            vmem(cache_values.shape, BF16),
            vmem(page_slot.shape, jnp.int32),
            vmem(decode_states.shape, BF16),
            pltpu.SMEM((rows,), jnp.int32),
            vmem((ranks, PAGE, pages), F32),
            vmem((ranks, PAGE, block), F32),
            vmem((ranks, PAGE, HEAD_WIDTH), F32),
            vmem((ranks, PAGE, HEAD_WIDTH), F32),
            vmem((pages, 4 * HEAD_WIDTH), BF16),
            vmem((groups, local_heads, HEAD_WIDTH), F32),
            vmem((groups, local_heads, HEAD_WIDTH), F32),
            vmem((ranks, rows * local_heads, HEAD_WIDTH), BF16),
            vmem((ranks, groups * local_heads, HEAD_WIDTH), BF16),
            vmem((heads // FOLD, rows + groups, FOLD, 2 * HEAD_WIDTH), BF16),
            vmem((tokens, kv_width), BF16),
            vmem((2, CHUNKS, chips, local_heads, chunk), F32),
            vmem((CHUNKS, chips, local_heads, chunk), F32),
            vmem((CHUNKS, chips, FOLD, local_heads * chunk // FOLD), BF16),
            vmem((CHUNKS, chips, FOLD, local_heads * chunk // FOLD), BF16),
            vmem((CHUNKS, local_heads, chunk), F32),
            vmem((ranks, FOLD, widths[0]), BF16),
            vmem((ranks, FOLD, widths[1]), BF16),
            vmem((groups * heads, longest), BF16),
            vmem((groups * heads, features), BF16),
            vmem((groups * ranks, FOLD, HEAD_WIDTH), F32),
            vmem((groups * ranks, FOLD, HEAD_WIDTH), BF16),
            vmem((groups * ranks, FOLD, HEAD_WIDTH), BF16),
            vmem((ranks, rows * local_heads, HEAD_WIDTH), F32),
            vmem((ranks, rows * local_heads, HEAD_WIDTH), BF16),
            vmem((ranks, rows * local_heads, HEAD_WIDTH), BF16),
            vmem((ranks, local_heads, HEAD_WIDTH), F32),
            vmem((ranks, local_heads, HEAD_WIDTH), F32),
            vmem((groups, PARTS, local_heads, HEAD_WIDTH), F32),
            vmem((groups, PARTS, local_heads, HEAD_WIDTH), F32),
            dma((ranks,)), dma((7,)), dma((PIECES,)),
            dma, dma, dma, dma, dma, dma, dma, dma,
            dma, dma((CHUNKS,)), dma, dma((CHUNKS,)),
            dma((PARTS,)), dma((PARTS,)), dma((PARTS,)), dma((PARTS,)),
            dma, dma, dma, dma, dma, dma, dma, dma,
        ],
        compiler_params=pltpu.CompilerParams(
            collective_id=0, has_side_effects=True, vmem_limit_bytes=58 * 1024 * 1024
        ),
    )(
        prefill_states, key_weight, value_weight, page_slot, decode_states, query_weight,
        cache_keys, cache_values, cached_length,
    )
    return result.reshape(rows, local_heads * HEAD_WIDTH)


def solution(mesh):
    placed = (
        P("group", "tensor"),
        P("tensor", None),
        P("tensor", None),
        P("group", "tensor", None),
        P("group", None),
        P(None, "tensor"),
        P("group", "tensor", None),
        P("group", "tensor", None),
        P("group"),
    )
    return jax.shard_map(
        per_device, mesh=mesh, in_specs=placed, out_specs=P("group", "tensor"), check_vma=False
    )
```

```python
import functools
import math

import jax
import jax.numpy as jnp
from jax import lax
from jax.experimental import pallas as pl
from jax.experimental.pallas import tpu as pltpu
from jax.sharding import PartitionSpec as P

HEAD_WIDTH = 128
PAGE = 8
FOLD = 16
CHUNKS = 4
PARTS = 2
BOUNDS = (0, 2, 4)
PIECES = 4

rope_theta = 500000.0
masked_score = -1e30
F32, BF16 = jnp.float32, jnp.bfloat16


def log2_of(number):
    power = number.bit_length() - 1
    assert 1 << power == number
    return power


def remote(src, dst, send_sem, recv_sem, group, rank):
    return pltpu.make_async_remote_copy(
        src_ref=src,
        dst_ref=dst,
        send_sem=send_sem,
        recv_sem=recv_sem,
        device_id={"group": group, "tensor": rank},
        device_id_type=pl.DeviceIdType.MESH,
    )


def stack(pieces):
    return pieces[0] if len(pieces) == 1 else jnp.concatenate(pieces, axis=0)


def beside(pieces):
    return pieces[0] if len(pieces) == 1 else jnp.concatenate(pieces, axis=1)


def fold(values):
    count = FOLD // values.shape[0]
    width = values.shape[1] // count
    return stack([values[:, q * width : (q + 1) * width] for q in range(count)])


def unfold(values, height):
    return beside([values[q : q + height] for q in range(0, FOLD, height)])


def iota(shape, axis):
    return lax.broadcasted_iota(jnp.int32, shape, axis)


def body(
    groups, ranks,
    states, key_weight, value_weight, page_slot, decode, query_weight, cache_keys, cache_values,
    cached_length,
    out,
    x, wk, wv, wq, old_keys, old_values, slot_in, decode_in, lengths,
    slots, slot_of, step_cos, step_sin, page_table, far_out, far_in,
    query_all, far_all, spread, keys,
    partial, paired, chip_sums, incoming, own_sums,
    weights_0, weights_1, masked, mixed, fresh_wide, fresh_out, fresh_in,
    old_wide, old_out, old_in, old_stat_out, old_stat_in, cross_out, cross_in,
    x_sems, load_sems, wq_sems,
    send_slot, got_slot, send_far, got_far, send_query, got_query, send_near, got_near,
    send_pair, got_pair, send_sum, got_sum, send_weight, got_weight, send_on, got_on,
    send_fresh, got_fresh, send_old, got_old, send_stat, got_stat, send_cross, got_cross,
):
    group, rank = lax.axis_index("group"), lax.axis_index("tensor")
    chips = ranks // 2
    core, chip = lax.rem(rank, 2), rank // 2
    partner = chip * 2 + 1 - core
    own = group * ranks + rank
    tokens, features = x.shape
    block = tokens // ranks
    pages = block // PAGE
    per_owner = pages // groups
    rows, context_dev, kv_width = old_keys.shape
    kv_heads = kv_width // HEAD_WIDTH
    local_heads = out.shape[1]
    heads = local_heads * ranks
    per_kv = heads // kv_heads
    share, span = block // groups, block // rows
    senders = span // share
    offset = lax.rem(group, senders) * share
    query_rows = 2 * rows
    depth = wq.shape[0] // PIECES
    weights = (weights_0, weights_1)
    chunk = tokens // CHUNKS
    per_chunk = chunk // block
    two_heads = 2 * HEAD_WIDTH
    assert FOLD == 2 * per_kv
    log_scale = math.log2(math.e) / HEAD_WIDTH**0.5
    half = HEAD_WIDTH // 2

    def rank_at(step):
        return lax.rem(rank + step, ranks)

    def group_at(step):
        return lax.rem(group + step, groups)

    def chip_at(step):
        other = lax.rem(chip + step, chips)
        return other, other * 2 + core

    def x_copy(step):
        start = pl.ds(pl.multiple_of(step * block, block), block)
        return pltpu.make_async_copy(states.at[start, :], x.at[start, :], x_sems.at[step])

    def query_load(i):
        span_i = pl.ds(i * depth, depth)
        return pltpu.make_async_copy(query_weight.at[span_i, :], wq.at[span_i, :], wq_sems.at[i])

    def load(source, target, index):
        return pltpu.make_async_copy(source, target, load_sems.at[index])

    key_load = load(key_weight, wk, 0)
    slot_load = load(page_slot, slot_in, 1)
    decode_load = load(decode, decode_in, 2)
    length_load = load(cached_length, lengths, 3)
    value_load = load(value_weight, wv, 4)
    old_key_load = load(cache_keys, old_keys, 5)
    old_value_load = load(cache_values, old_values, 6)

    slot_load.start()
    decode_load.start()
    length_load.start()
    key_load.start()
    x_copy(rank).start()
    query_load(0).start()

    barrier = pltpu.get_barrier_semaphore()

    def greet(peer_group, peer_rank):
        pl.semaphore_signal(
            barrier,
            inc=1,
            device_id={"group": peer_group, "tensor": peer_rank},
            device_id_type=pl.DeviceIdType.MESH,
        )

    for step in range(1, groups):
        greet(group_at(step), rank)
    for step in range(1, ranks):
        greet(group, rank_at(step))

    def slot_copy(step):
        return remote(
            slots.at[rank], slots.at[rank], send_slot, got_slot,
            group, rank_at(step),
        )

    def far_copy(step):
        peer = group_at(step)
        return remote(
            far_out.at[peer], far_in.at[group], send_far, got_far, peer, rank
        )

    def near_copy(step):
        return remote(
            far_all.at[rank], far_all.at[rank], send_near, got_near,
            group, rank_at(step),
        )

    def query_copy(step):
        return remote(
            query_all.at[rank], query_all.at[rank], send_query, got_query,
            group, rank_at(step),
        )

    def pair_copy(c):
        return remote(
            partial.at[1 - core, c], paired.at[c], send_pair, got_pair.at[c], group, partner
        )

    def sum_copy(step, c):
        other, peer = chip_at(step)
        return remote(
            chip_sums.at[c, other], incoming.at[c, chip], send_sum, got_sum.at[c], group, peer,
        )

    def weight_copy(step, p):
        other, peer = chip_at(step)
        return remote(
            weights[p].at[rank], weights[p].at[rank], send_weight.at[p],
            got_weight.at[p], group, peer,
        )

    def on_copy(step, p):
        other, peer = chip_at(step)
        return remote(
            weights[p].at[peer], weights[p].at[peer], send_on.at[p],
            got_on.at[p], group, partner,
        )

    def other_at(step):
        peer = lax.rem(own + step, groups * ranks)
        return peer // ranks, lax.rem(peer, ranks)

    def fresh_copy(peer):
        return remote(
            fresh_out.at[peer], fresh_in.at[own], send_fresh, got_fresh,
            peer // ranks, lax.rem(peer, ranks),
        )

    def old_copies(step):
        peer = rank_at(step)
        return (
            remote(
                old_out.at[peer], old_in.at[rank], send_old, got_old, group, peer
            ),
            remote(
                old_stat_out.at[peer], old_stat_in.at[rank], send_stat, got_stat, group, peer,
            ),
        )

    def cross_copy(step):
        peer = group_at(step)
        return remote(
            cross_out.at[peer], cross_in.at[group], send_cross, got_cross,
            peer, rank,
        )

    def arrived(ref, semaphore):
        remote(ref, ref, semaphore, semaphore, group, partner).wait_recv()

    def left(ref, semaphore):
        remote(ref, ref, semaphore, semaphore, group, partner).wait_send()

    other_ranks, other_groups = pl.ds(1, ranks - 1), pl.ds(1, groups - 1)
    other_chips = pl.ds(1, chips - 1)

    lane = iota((1, HEAD_WIDTH), 1)
    sign = jnp.where(lane < half, -1.0, 1.0).astype(F32)
    frequency = jnp.exp(
        jnp.where(lane < half, lane, lane - half).astype(F32)
        * (-2.0 * math.log(rope_theta) / HEAD_WIDTH)
    )
    line = iota((ranks * PAGE, HEAD_WIDTH), 0)
    start = (line >> log2_of(PAGE)) * span + (line & (PAGE - 1)) + offset
    step_angle = start.astype(F32) * frequency
    step_cos[...] = jnp.cos(step_angle).reshape(step_cos.shape)
    step_sin[...] = jnp.sin(step_angle).reshape(step_sin.shape)
    line = iota((pages, HEAD_WIDTH), 0)
    page_angle = ((line & (per_owner - 1)) * PAGE).astype(F32) * frequency
    for i, table in enumerate((jnp.cos(page_angle), jnp.sin(page_angle))):
        high = table.astype(BF16)
        page_table[:, 2 * i * HEAD_WIDTH : (2 * i + 1) * HEAD_WIDTH] = high
        page_table[:, (2 * i + 1) * HEAD_WIDTH : (2 * i + 2) * HEAD_WIDTH] = (
            table - high.astype(F32)
        ).astype(BF16)
    slot_load.wait()
    slots[rank] = jnp.broadcast_to(slot_in[0].astype(F32), (PAGE, pages))
    length_load.wait()
    query_row = iota((query_rows, HEAD_WIDTH), 0)
    position = jnp.zeros((query_rows, HEAD_WIDTH), jnp.int32)
    for b in range(rows):
        position = jnp.where(query_row == b, lengths[b], position)
    query_angle = (position + ranks * span).astype(F32) * frequency
    query_cos, query_sin = jnp.cos(query_angle), jnp.sin(query_angle) * sign
    on_diagonal = iota((pages, pages), 0) == iota((pages, pages), 1)
    page_lane = iota((pages, pages), 1).astype(F32)

    def project_keys(t):
        tokens_t = pl.ds(pl.multiple_of(t * block, block), block)
        row = jnp.broadcast_to(slots[t][0:1], (pages, pages))
        column = jnp.sum(jnp.where(on_diagonal, row, 0.0), axis=1, keepdims=True)
        chosen = jnp.where(page_lane == column, 1.0, 0.0).astype(BF16)
        table = jnp.dot(chosen, page_table[...], preferred_element_type=F32)
        big_cos = (table[:, :HEAD_WIDTH] + table[:, HEAD_WIDTH : 2 * HEAD_WIDTH]).reshape(
            pages, 1, HEAD_WIDTH
        )
        big_sin = (
            table[:, 2 * HEAD_WIDTH : 3 * HEAD_WIDTH] + table[:, 3 * HEAD_WIDTH :]
        ).reshape(pages, 1, HEAD_WIDTH)
        small_cos = step_cos[t].reshape(1, PAGE, HEAD_WIDTH)
        small_sin = step_sin[t].reshape(1, PAGE, HEAD_WIDTH)
        cosine = (big_cos * small_cos - big_sin * small_sin).reshape(block, HEAD_WIDTH)
        sine = (big_sin * small_cos + big_cos * small_sin).reshape(block, HEAD_WIDTH) * sign
        wide = 2 * HEAD_WIDTH
        for n in range(kv_width // wide):
            found = jnp.dot(
                x[tokens_t, :], wk[:, n * wide : (n + 1) * wide], preferred_element_type=F32
            )
            for i in range(2):
                head = found[:, i * HEAD_WIDTH : (i + 1) * HEAD_WIDTH]
                start = n * wide + i * HEAD_WIDTH
                keys[tokens_t, start : start + HEAD_WIDTH] = (
                    head * cosine + pltpu.roll(head, half, 1) * sine
                ).astype(BF16)

    def turn_near():
        arrived(far_in.at[other_groups], got_far)
        far_all[rank] = stack([far_in[o] for o in range(groups)]).astype(BF16)
        for step in range(1, ranks):
            near_copy(step).start()

    def spread_queries():
        arrived(far_all.at[other_ranks], got_near)
        arrived(query_all.at[other_ranks], got_query)
        per_tile = FOLD // local_heads
        for r in range(rows + groups):
            held, at = (query_all, r) if r < rows else (far_all, r - rows)
            for u in range(heads // FOLD):
                members = range(u * per_tile, (u + 1) * per_tile)
                taken = [
                    held[j].astype(F32)[at * local_heads : (at + 1) * local_heads]
                    for j in members
                ]
                for h in sorted({j * local_heads // per_kv for j in members}):
                    first = h * HEAD_WIDTH - u * two_heads
                    spread[u, r, :, first : first + HEAD_WIDTH] = stack(
                        [
                            value if j * local_heads // per_kv == h else jnp.zeros_like(value)
                            for j, value in zip(members, taken)
                        ]
                    ).astype(BF16)

    def add_pair(c):
        arrived(paired.at[c], got_pair.at[c])
        for k in range(chips):
            chip_sums[c, k] = fold(partial[core, c, k] + paired[c, k]).astype(BF16)
        for step in range(1, chips):
            sum_copy(step, c).start()
        own_sums[c] = partial[core, c, chip] + paired[c, chip]

    nt = (((1,), (1,)), ((), ()))

    def score(first, c, carry):
        for u in range(per_chunk):
            t = c * per_chunk + u
            slot = slot_of[t][0:1]
            for n in range(heads // FOLD):
                found = lax.dot_general(
                    spread[n, rows:].reshape(groups * FOLD, two_heads),
                    keys[
                        pl.ds(pl.multiple_of(t * block, block), block),
                        n * two_heads : (n + 1) * two_heads,
                    ],
                    nt,
                    preferred_element_type=F32,
                )
                kept = found[:FOLD]
                for o in range(1, groups):
                    kept = jnp.where(
                        slot >= o * per_owner, found[o * FOLD : (o + 1) * FOLD], kept
                    )
                for i in range(FOLD // local_heads):
                    j = n * (FOLD // local_heads) + i
                    partial[j % 2, c, j // 2, :, u * block : (u + 1) * block] = kept[
                        i * local_heads : (i + 1) * local_heads
                    ]
        pair_copy(c).start()

        @pl.when(c > first)
        def _():
            add_pair(c - 1)

        return carry

    def block_at(tick):
        return jnp.where(tick - 1 < rank, tick - 1, tick)

    key_load.wait()
    x_copy(rank).wait()
    for i in range(1, PIECES):
        query_load(i).start()
    project_keys(rank)
    pl.semaphore_wait(barrier, groups + ranks - 2)
    for step in range(1, ranks):
        slot_copy(step).start()
    decode_load.wait()
    turns = depth // min(depth, 1024)

    def add_piece(i, total):
        span_i = pl.ds(pl.multiple_of(i * (depth // turns), depth // turns), depth // turns)
        return total + jnp.dot(
            decode_in[:, span_i], wq[span_i, :], preferred_element_type=F32
        )

    total = jnp.zeros((rows, wq.shape[1]), F32)
    for i in range(PIECES):
        query_load(i).wait()
        total = lax.fori_loop(i * turns, (i + 1) * turns, add_piece, total)
        if i == PIECES - 2:
            for tick in range(1, ranks):
                x_copy(block_at(tick)).start()
    total = stack([total, total])
    turned = []
    for h in range(local_heads):
        head = total[:, h * HEAD_WIDTH : (h + 1) * HEAD_WIDTH]
        turned.append(head * query_cos + pltpu.roll(head, half, 1) * query_sin)
    size = local_heads * query_rows
    m, k = iota((size, size), 0), iota((size, size), 1)
    order = (m >> log2_of(local_heads) == k & (query_rows - 1)) & (
        m & (local_heads - 1) == k >> log2_of(query_rows)
    )
    arranged = jnp.dot(
        jnp.where(order, 1.0, 0.0).astype(BF16),
        stack(turned).astype(BF16),
        preferred_element_type=F32,
    )
    for g in range(groups):
        at = (rows + g // senders) * local_heads
        far_out[g] = arranged[at : at + local_heads]
    for step in range(1, groups):
        far_copy(step).start()
    query_all[rank] = arranged[: rows * local_heads].astype(BF16)
    for step in range(1, ranks):
        query_copy(step).start()
    far_in[group] = far_out[group]
    value_load.start()
    old_key_load.start()
    old_value_load.start()
    arrived(slots.at[other_ranks], got_slot)
    widen = (
        (iota((pages, block), 1) >> log2_of(PAGE)) == iota((pages, block), 0)
    ).astype(BF16)
    slot_of[...] = jnp.dot(
        slots[...].reshape(ranks * PAGE, pages).astype(BF16), widen, preferred_element_type=F32
    ).reshape(ranks, PAGE, block)

    near_tick, score_tick = 3 * ranks // 8, ranks - 3

    def scored(tick):
        ready = jnp.where(tick == ranks - 1, CHUNKS, tick // per_chunk)
        return jnp.where(tick < score_tick, 0, ready)

    def project(tick, carry):
        @pl.when(tick == near_tick)
        def _():
            turn_near()

        t = block_at(tick)
        x_copy(t).wait()
        project_keys(t)
        before, first, last = scored(tick - 2), scored(tick - 1), scored(tick)

        @pl.when(first > before)
        def _():
            add_pair(first - 1)

        @pl.when(tick == score_tick)
        def _():
            spread_queries()

        lax.fori_loop(first, last, functools.partial(score, first), 0)
        return carry

    lax.fori_loop(1, ranks, project, 0)

    def attend_old(b):
        found = stack(
            [
                lax.dot_general(
                    spread[n, b],
                    old_keys[b, :, n * two_heads : (n + 1) * two_heads],
                    nt,
                    preferred_element_type=F32,
                )
                for n in range(heads // FOLD)
            ]
        )
        place = rank * context_dev + iota((1, context_dev), 1)
        found = jnp.where(place < lengths[b], found, masked_score)
        peak = jnp.max(found, axis=-1, keepdims=True)
        exact = jnp.exp2((found - peak) * log_scale)
        amount = jnp.sum(exact, axis=-1, keepdims=True)
        exact = exact.astype(BF16)
        for n in range(heads // FOLD):
            summed = jnp.dot(
                exact[n * FOLD : (n + 1) * FOLD],
                old_values[b, :, n * two_heads : (n + 1) * two_heads],
                preferred_element_type=F32,
            )
            for i in range(FOLD // local_heads):
                h = i * local_heads // per_kv
                old_wide[
                    n * (FOLD // local_heads) + i, b * local_heads : (b + 1) * local_heads
                ] = summed[
                    i * local_heads : (i + 1) * local_heads,
                    h * HEAD_WIDTH : (h + 1) * HEAD_WIDTH,
                ]
        return jnp.where(lane == b, peak * log_scale, jnp.where(lane == rows + b, amount, 0.0))

    def softmax(p):
        sums = []
        for c in range(BOUNDS[p], BOUNDS[p + 1]):
            total = own_sums[c]
            arrived(incoming.at[c, other_chips], got_sum.at[c])
            for step in range(1, chips):
                other = chip_at(step)[0]
                total = total + unfold(incoming[c, other].astype(F32), local_heads)
            sums.append(total)
        total = beside(sums)
        slot = beside(
            [
                slot_of[t][:local_heads]
                for t in range(BOUNDS[p] * per_chunk, BOUNDS[p + 1] * per_chunk)
            ]
        )
        peak_of, peaks = jnp.zeros_like(total), []
        for o in range(groups):
            owned = (slot >= o * per_owner) & (slot < (o + 1) * per_owner)
            peak = jnp.max(jnp.where(owned, total, masked_score), axis=-1, keepdims=True)
            peak_of = jnp.where(owned, peak, peak_of)
            peaks.append(peak * log_scale)
        exact = jnp.exp2((total - peak_of) * log_scale)
        weights[p][rank] = fold(exact).astype(BF16)
        for step in range(1, chips):
            weight_copy(step, p).start()
        on_copy(0, p).start()
        for o in range(groups):
            owned = (slot >= o * per_owner) & (slot < (o + 1) * per_owner)
            amount = jnp.sum(jnp.where(owned, exact, 0.0), axis=-1, keepdims=True)
            cross_out[o, p] = jnp.where(lane < half, peaks[o], amount)

    def pass_on(p):
        arrived(weights[p].at[other_chips], got_weight.at[p])
        for step in range(1, chips):
            on_copy(step, p).start()

    def mix(p):
        arrived(weights[p].at[pl.ds(0, chips)], got_on.at[p])
        width = weights[p].shape[2]
        base = BOUNDS[p] * chunk
        part = (BOUNDS[p + 1] - BOUNDS[p]) * chunk
        for q in range(FOLD // local_heads):
            every = stack(
                [
                    weights[p][j].astype(F32)[q * local_heads : (q + 1) * local_heads]
                    for j in range(ranks)
                ]
            )
            for u in range(width // block):
                start = q * width + u * block
                slot = slot_of[(base + start) // block][0:1]
                values = every[:, u * block : (u + 1) * block]
                for o in range(groups):
                    owned = (slot >= o * per_owner) & (slot < (o + 1) * per_owner)
                    masked[o * heads : (o + 1) * heads, start : start + block] = jnp.where(
                        owned, values, 0.0
                    ).astype(BF16)
        wide = 2 * HEAD_WIDTH
        for n in range(features // wide):
            mixed[:, n * wide : (n + 1) * wide] = jnp.dot(
                masked[:, :part],
                x[base : base + part, n * wide : (n + 1) * wide],
                preferred_element_type=F32,
            ).astype(BF16)
        tall = 2 * per_kv
        for n in range(kv_heads // 2):
            left = stack(
                [
                    mixed[o * heads + n * tall : o * heads + (n + 1) * tall, :]
                    for o in range(groups)
                ]
            )
            found = jnp.dot(left, wv[:, n * wide : (n + 1) * wide], preferred_element_type=F32)
            for i in range(tall // local_heads):
                h = i * local_heads // per_kv
                first = p * (FOLD // PARTS)
                for o in range(groups):
                    at = o * tall + i * local_heads
                    fresh_wide[o * ranks + n * (tall // local_heads) + i, first : first + local_heads] = found[
                        at : at + local_heads, h * HEAD_WIDTH : (h + 1) * HEAD_WIDTH
                    ]
            if p == PARTS - 1:
                count = tall // local_heads

                def send(index, carry):
                    peer = index // count * ranks + n * count + lax.rem(index, count)
                    fresh_out[peer] = fresh_wide[peer].astype(BF16)

                    @pl.when(peer != own)
                    def _():
                        fresh_copy(peer).start()

                    return carry

                lax.fori_loop(0, groups * count, send, 0)

    add_pair(CHUNKS - 1)
    old_key_load.wait()
    old_value_load.wait()
    about = attend_old(0)
    for b in range(1, rows // 2):
        about = about + attend_old(b)
    softmax(0)
    for b in range(rows // 2, rows):
        about = about + attend_old(b)
    softmax(1)
    for step in range(1, groups):
        cross_copy(step).start()
    cross_in[group] = cross_out[group]
    for j in range(ranks):
        old_out[j] = old_wide[j].astype(BF16)
        old_stat_out[j] = about[j * local_heads : (j + 1) * local_heads]
    pass_on(0)
    pass_on(1)
    for step in range(1, ranks):
        for copy in old_copies(step):
            copy.start()
    value_load.wait()
    mix(0)
    mix(1)
    fresh_in[own] = fresh_out[own]

    old_in[rank] = old_out[rank]
    old_stat_in[rank] = old_stat_out[rank]
    arrived(old_in.at[other_ranks], got_old)
    arrived(old_stat_in.at[other_ranks], got_stat)
    held = []
    for b in range(rows):
        tops = [old_stat_in[r][:, b : b + 1] for r in range(ranks)]
        top = functools.reduce(jnp.maximum, tops)
        numerator, denominator = 0.0, 0.0
        for r in range(ranks):
            factor = jnp.exp2(tops[r] - top)
            numerator = numerator + factor * old_in[r].astype(F32)[
                b * local_heads : (b + 1) * local_heads
            ]
            denominator = denominator + factor * old_stat_in[r][:, rows + b : rows + b + 1]
        held.append((top, numerator, denominator))

    arrived(cross_in.at[other_groups], got_cross)
    found = [[item] for item in held]
    arrived(fresh_in.at[pl.ds(1, groups * ranks - 1)], got_fresh)
    for source in range(groups):
        total = jnp.sum(fresh_in[source * ranks : (source + 1) * ranks].astype(F32), axis=0)
        for p in range(PARTS):
            stat = cross_in[source, p]
            first = p * (FOLD // PARTS)
            found[source // senders].append(
                (stat[:, 0:1], total[first : first + local_heads], stat[:, half : half + 1])
            )
    for b in range(rows):
        top = functools.reduce(jnp.maximum, [item[0] for item in found[b]])
        numerator, denominator = 0.0, 0.0
        for peak, value, amount in found[b]:
            factor = jnp.exp2(peak - top)
            numerator = numerator + factor * value
            denominator = denominator + factor * amount
        out[b] = (numerator / denominator).astype(out.dtype)

    left(slots.at[other_ranks], send_slot)
    left(query_all.at[other_ranks], send_query)
    left(far_all.at[other_ranks], send_near)
    left(far_in.at[other_groups], send_far)
    left(old_in.at[other_ranks], send_old)
    left(old_stat_in.at[other_ranks], send_stat)
    left(cross_in.at[other_groups], send_cross)
    left(fresh_in.at[pl.ds(1, groups * ranks - 1)], send_fresh)
    left(paired, send_pair)
    left(incoming.at[:, other_chips], send_sum)
    for p in range(PARTS):
        left(weights[p].at[other_chips], send_weight.at[p])
        left(weights[p].at[pl.ds(0, chips)], send_on.at[p])


def per_device(
    prefill_states, key_weight, value_weight, page_slot, decode_states, query_weight,
    cache_keys, cache_values, cached_length,
):
    groups = lax.axis_size("group")
    ranks = lax.axis_size("tensor")
    chips = ranks // 2
    tokens, features = prefill_states.shape
    kv_width = key_weight.shape[1]
    block = tokens // ranks
    pages = block // PAGE
    rows, model = decode_states.shape
    width = query_weight.shape[1]
    local_heads = width // HEAD_WIDTH
    heads = local_heads * ranks
    chunk = tokens // CHUNKS
    widths = [
        local_heads * chunk * (BOUNDS[p + 1] - BOUNDS[p]) // FOLD for p in range(PARTS)
    ]
    longest = chunk * max(BOUNDS[p + 1] - BOUNDS[p] for p in range(PARTS))
    dma = pltpu.SemaphoreType.DMA
    vmem = pltpu.VMEM
    hbm = pl.BlockSpec(memory_space=pltpu.HBM)
    result = pl.pallas_call(
        functools.partial(body, groups, ranks),
        in_specs=[hbm] * 9,
        out_specs=pl.BlockSpec(memory_space=pltpu.VMEM),
        out_shape=jax.ShapeDtypeStruct((rows, local_heads, HEAD_WIDTH), BF16),
        scratch_shapes=[
            vmem((tokens, features), BF16),
            vmem((features, kv_width), BF16),
            vmem((features, kv_width), BF16),
            vmem(query_weight.shape, BF16),
            vmem(cache_keys.shape, BF16),
            vmem(cache_values.shape, BF16),
            vmem(page_slot.shape, jnp.int32),
            vmem(decode_states.shape, BF16),
            pltpu.SMEM((rows,), jnp.int32),
            vmem((ranks, PAGE, pages), F32),
            vmem((ranks, PAGE, block), F32),
            vmem((ranks, PAGE, HEAD_WIDTH), F32),
            vmem((ranks, PAGE, HEAD_WIDTH), F32),
            vmem((pages, 4 * HEAD_WIDTH), BF16),
            vmem((groups, local_heads, HEAD_WIDTH), F32),
            vmem((groups, local_heads, HEAD_WIDTH), F32),
            vmem((ranks, rows * local_heads, HEAD_WIDTH), BF16),
            vmem((ranks, groups * local_heads, HEAD_WIDTH), BF16),
            vmem((heads // FOLD, rows + groups, FOLD, 2 * HEAD_WIDTH), BF16),
            vmem((tokens, kv_width), BF16),
            vmem((2, CHUNKS, chips, local_heads, chunk), F32),
            vmem((CHUNKS, chips, local_heads, chunk), F32),
            vmem((CHUNKS, chips, FOLD, local_heads * chunk // FOLD), BF16),
            vmem((CHUNKS, chips, FOLD, local_heads * chunk // FOLD), BF16),
            vmem((CHUNKS, local_heads, chunk), F32),
            vmem((ranks, FOLD, widths[0]), BF16),
            vmem((ranks, FOLD, widths[1]), BF16),
            vmem((groups * heads, longest), BF16),
            vmem((groups * heads, features), BF16),
            vmem((groups * ranks, FOLD, HEAD_WIDTH), F32),
            vmem((groups * ranks, FOLD, HEAD_WIDTH), BF16),
            vmem((groups * ranks, FOLD, HEAD_WIDTH), BF16),
            vmem((ranks, rows * local_heads, HEAD_WIDTH), F32),
            vmem((ranks, rows * local_heads, HEAD_WIDTH), BF16),
            vmem((ranks, rows * local_heads, HEAD_WIDTH), BF16),
            vmem((ranks, local_heads, HEAD_WIDTH), F32),
            vmem((ranks, local_heads, HEAD_WIDTH), F32),
            vmem((groups, PARTS, local_heads, HEAD_WIDTH), F32),
            vmem((groups, PARTS, local_heads, HEAD_WIDTH), F32),
            dma((ranks,)), dma((7,)), dma((PIECES,)),
            dma, dma, dma, dma, dma, dma, dma, dma,
            dma, dma((CHUNKS,)), dma, dma((CHUNKS,)),
            dma((PARTS,)), dma((PARTS,)), dma((PARTS,)), dma((PARTS,)),
            dma, dma, dma, dma, dma, dma, dma, dma,
        ],
        compiler_params=pltpu.CompilerParams(
            collective_id=0, has_side_effects=True, vmem_limit_bytes=58 * 1024 * 1024
        ),
    )(
        prefill_states, key_weight, value_weight, page_slot, decode_states, query_weight,
        cache_keys, cache_values, cached_length,
    )
    return result.reshape(rows, local_heads * HEAD_WIDTH)


def solution(mesh):
    placed = (
        P("group", "tensor"),
        P("tensor", None),
        P("tensor", None),
        P("group", "tensor", None),
        P("group", None),
        P(None, "tensor"),
        P("group", "tensor", None),
        P("group", "tensor", None),
        P("group"),
    )
    return jax.shard_map(
        per_device, mesh=mesh, in_specs=placed, out_specs=P("group", "tensor"), check_vma=False
    )
```
